512 devices in a mesh: harm: 32 (over y_lo, z), slab: 16 (over y_hi, x, core).
Axes of the slice: x: 4, y: 8 (y_hi: 2, y_lo: 4; y = y_hi * 4 + y_lo), z: 8, core: 2. Of those that a mesh axis runs over, the one named last changes fastest.
Arguments:
- fields: bfloat16 [64, 4, 2, 5, 128, 256], P('harm', None, None, None, 'slab'), may hold values from -6 to 6
- base_store: bfloat16 [32, 2, 5, 128, 256], P('harm', None, None, 'slab'), may hold values from -3 to 3
- harmonic_index: int32 [3], replicated, may hold values from 1 to 63
- owners: int32 [3], replicated, may hold values from 0 to 31
- sponge_flags: int32 [128], P('slab'), may hold values 0 or 1
- mixing: float32 [5, 5], replicated, may hold values from -2.5 to 2.5
Outputs:
- applied: bfloat16 [64, 4, 2, 5, 128, 256], P('harm', None, None, None, 'slab')
The draws below stay inside these ranges and needn't reach their ends.
Inputs may be any that keep to these rules, and one draw needn't show every extreme that they name: `harmonic_index`: indices of the coupling base-flow harmonics, taken modulo 64.
All inputs are finite; a program needn't handle non-finite values. No bound on the sum of `sponge_flags` on one device may be relied on, other than what follows from the above.
Results may differ from the reference program's by a relative error of at most 0.0075.
Values may be sent and summed in bfloat16 or wider, within the bound.
A program may use at most 64 MiB of HBM per device.

```python
import jax
import jax.numpy as jnp
from jax import lax

NH = 64
NVAR = 5
NC = 4
NBASE = 3
NYZ = 256
NX = 128
N_HARM = 32


def place_ends(values, rng, smallest, largest):
    extent = values.shape
    spot = [jax.random.randint(jax.random.fold_in(rng, axis), (), 0, extent[axis]) for axis in range(len(extent))]
    values = values.at[tuple(spot)].set(smallest)
    longest = extent.index(max(extent))
    spot[longest] = (spot[longest] + 1) % extent[longest]
    return values.at[tuple(spot)].set(largest)


def levels(stream_key, extent, pieces, low, top_value):
    factor_of = 1.0
    for axis_at, shards_of in pieces:
        steps = jax.random.uniform(jax.random.fold_in(jax.random.fold_in(stream_key, 6), axis_at), (shards_of,), jnp.float32, low / len(pieces), top_value / len(pieces))
        factor_of = factor_of * jnp.repeat(jnp.exp(steps), extent[axis_at] // shards_of).reshape((-1,) + (1,) * (len(extent) - 1 - axis_at))
    return factor_of


def scatter_about(rng, shape, width, most, pieces=(), kind=jnp.bfloat16):
    values = width * jax.random.normal(rng, shape, jnp.float32)
    if pieces:
        values = values * levels(rng, shape, pieces, -0.22, 0.18)
    return jnp.clip(values, -most, most).astype(kind)


def setup_inputs(seed: int = 0) -> dict:
    splits = jax.random.split(jax.random.key(seed), 7)
    fields = scatter_about(splits[0], (NH, NC, 2, NVAR, NX, NYZ), 1.0, 6.0, ((0, 32), (4, 16)))
    base_store = scatter_about(splits[1], (N_HARM, 2, NVAR, NX, NYZ), 0.5, 3.0, ((0, 32), (3, 16)))
    harmonic_index = jax.random.randint(splits[2], (NBASE,), 1, NH).astype(jnp.int32)
    owners = jax.random.randint(splits[3], (NBASE,), 0, N_HARM).astype(jnp.int32)
    sponge_flags = place_ends((jax.random.randint(splits[4], (NX,), 0, 4) < 1).astype(jnp.int32), jax.random.fold_in(splits[4], 1), 0, 1)
    mixing = scatter_about(splits[5], (NVAR, NVAR), NVAR ** -0.5, 2.5, (), jnp.float32)
    return {"fields": fields, "base_store": base_store, "harmonic_index": harmonic_index, "owners": owners, "sponge_flags": sponge_flags, "mixing": mixing}


coeffs = (0.75, -0.15, 1.0 / 60.0)


def gradient(src):
    total = jnp.zeros(src.shape, jnp.float32)
    for shift_by in range(1, 4):
        weight = coeffs[shift_by - 1]
        total = total + weight * (jnp.roll(src, -shift_by, axis=3) - jnp.roll(src, shift_by, axis=3))
        total = total + weight * (jnp.roll(src, -shift_by, axis=4) - jnp.roll(src, shift_by, axis=4))
    return total


def reference(fields, base_store, harmonic_index, owners, sponge_flags, mixing):
    bases = [base_store[owners[j]].astype(jnp.float32) for j in range(NBASE)]
    flags = sponge_flags.astype(jnp.float32).reshape((NX, 1))

    def mix_one(index):
        src = lax.dynamic_index_in_dim(fields, index, 0, keepdims=False).astype(jnp.float32)
        mixed = jnp.einsum('vw,cpwxz->cpvxz', mixing, gradient(src), precision=lax.Precision.HIGHEST)
        return mixed.astype(jnp.bfloat16)

    mixed_all = lax.map(mix_one, jnp.arange(NH, dtype=jnp.int32))

    def one_harmonic(index):
        local = lax.dynamic_index_in_dim(fields, index, 0, keepdims=False).astype(jnp.float32)
        freq = 0.1 * jnp.where(index < NH // 2, index, index - NH).astype(jnp.float32)
        real_part = -freq * local[:, 1] - 2.0 * flags * local[:, 0]
        imag_part = freq * local[:, 0] - 2.0 * flags * local[:, 1]
        for j in range(NBASE):
            source_index = ((index - harmonic_index[j]) % NH).astype(jnp.int32)
            mixed = lax.dynamic_index_in_dim(mixed_all, source_index, 0, keepdims=False).astype(jnp.float32)
            base_real, base_imag = bases[j][0], bases[j][1]
            real_part = real_part + base_real * mixed[:, 0] - base_imag * mixed[:, 1]
            imag_part = imag_part + base_real * mixed[:, 1] + base_imag * mixed[:, 0]
        return jnp.stack([real_part, imag_part], axis=1).astype(jnp.bfloat16)

    return lax.map(one_harmonic, jnp.arange(NH, dtype=jnp.int32))
```

```python
import jax
import jax.numpy as jnp
from jax import lax
from jax.experimental import pallas as pl
from jax.experimental.pallas import tpu as pltpu
from jax.sharding import PartitionSpec as P

COEFFS = (0.75, -0.15, 1.0 / 60.0)
NBASE = 3
NCOL = 4
NVAR = 5
CHUNKS = 8
MESH = pl.DeviceIdType.MESH
BF = jnp.bfloat16
F32 = jnp.float32


def build(NY, NZ, NS, interpret=False):
    NT = 2 * NZ
    NH = NY * NT
    HA = NZ // 2
    HB = NZ // 2 - 1
    NO = NY - 1
    RING = CHUNKS + 1
    inject = [0] + [1, 1, 2, 3, 4, 5, 6, 7]

    def kernel(f_hbm, b_hbm, hidx, own, flg, mix, o_hbm, f, bown, hs, hr, gb, qr, bb, *rest):
        g = rest[:CHUNKS]
        (ps, pr, acc, ob, ld_sem, h_send, h_recv, a_send, a_recv, b_send, b_recv, y_send, y_recv,
         x_send, x_recv, p_send, p_recv, o_sem) = rest[CHUNKS:]
        me = lax.axis_index("harm")
        slab = lax.axis_index("slab")
        y, z = me // NZ, me % NZ
        zside = (y * NZ + (z + 1) % NZ, y * NZ + (z + NZ - 1) % NZ)
        yside = [((y + o) % NY) * NZ + z for o in range(1, NY)]
        sside = ((slab + 1) % NS, (slab + NS - 1) % NS)

        loads = [pltpu.make_async_copy(b_hbm.at[0], bown, ld_sem.at[NCOL])]
        loads += [pltpu.make_async_copy(f_hbm.at[:, c], f.at[:, c], ld_sem.at[c]) for c in range(NCOL)]
        for load in loads:
            load.start()

        barrier = pltpu.get_barrier_semaphore()
        for n in zside:
            pl.semaphore_signal(barrier, inc=1, device_id={"harm": n}, device_id_type=MESH)
        for n in yside:
            pl.semaphore_signal(barrier, inc=1, device_id={"harm": n}, device_id_type=MESH)
        for n in sside:
            pl.semaphore_signal(barrier, inc=1, device_id={"slab": n}, device_id_type=MESH)

        row = lax.broadcasted_iota(jnp.int32, (8, 256), 0)

        def pack(c):
            def one(i, _):
                for v in range(NVAR):
                    re = f[i, c, 0, v].astype(F32)
                    im = f[i, c, 1, v].astype(F32)
                    hs[0, c, i, v] = jnp.where(row < 4, pltpu.roll(re, 4, 0), im).astype(BF)
                    hs[1, c, i, v] = jnp.where(row < 4, re, pltpu.roll(im, 4, 0)).astype(BF)
                return 0

            lax.fori_loop(0, 2, one, 0)

        loads[0].wait()
        for half in range(2):
            for r in range(2):
                for v in range(NVAR):
                    gb[z, half, r, v] = bown[r, v, :, 128 * half : 128 * half + 128]
        for c in range(NCOL):
            loads[1 + c].wait()
            pack(c)

        pl.semaphore_wait(barrier, 2 + NO + 2)

        def halo(d, c):
            return pltpu.make_async_remote_copy(
                hs.at[d, c], hr.at[d, c], h_send.at[d, c], h_recv.at[d, c],
                device_id={"slab": sside[d]}, device_id_type=MESH)

        def ring(k, way, hop):
            sign = 1 if (k + way) % 2 == 0 else -1
            origin = (z + NZ - sign * (hop - 1)) % NZ
            buf = gb if k == 0 else g[k - 1]
            send, recv = (a_send, a_recv) if way == 0 else (b_send, b_recv)
            return pltpu.make_async_remote_copy(
                buf.at[origin], buf.at[origin], send.at[k, hop - 1], recv.at[k, hop - 1],
                device_id={"harm": zside[0 if sign == 1 else 1]}, device_id_type=MESH)

        def ring_arrived(k, way, hop):
            sign = 1 if (k + way) % 2 == 0 else -1
            origin = (z + NZ - sign * hop) % NZ
            buf = gb if k == 0 else g[k - 1]
            send, recv = (a_send, a_recv) if way == 0 else (b_send, b_recv)
            pltpu.make_async_remote_copy(
                buf.at[origin], buf.at[origin], send.at[k, hop - 1], recv.at[k, hop - 1],
                device_id={"harm": zside[0 if sign == 1 else 1]}, device_id_type=MESH).wait_recv()

        def base_row(o):
            return pltpu.make_async_remote_copy(
                qr.at[y], qr.at[y], y_send.at[o - 1], y_recv.at[o - 1],
                device_id={"harm": yside[o - 1]}, device_id_type=MESH)

        def base_row_arrived(o):
            src = (y + NY - o) % NY
            pltpu.make_async_remote_copy(
                qr.at[src], qr.at[src], y_send.at[o - 1], y_recv.at[o - 1],
                device_id={"harm": yside[o - 1]}, device_id_type=MESH).wait_recv()

        w = z % 2
        pair = y * NZ + z + 1 - 2 * w

        def base_pair(slot):
            return pltpu.make_async_remote_copy(
                bb.at[slot], bb.at[slot], x_send.at[0], x_recv.at[0],
                device_id={"harm": pair}, device_id_type=MESH)

        def part(q, o):
            return pltpu.make_async_remote_copy(
                ps.at[q, o - 1], pr.at[q, o - 1], p_send.at[q, o - 1], p_recv.at[q, o - 1],
                device_id={"harm": yside[o - 1]}, device_id_type=MESH)

        def out_copy(c):
            return pltpu.make_async_copy(ob.at[:, c], o_hbm.at[:, c], o_sem.at[c])

        def mixed(c):
            weights = [[mix[v, u] for u in range(NVAR)] for v in range(NVAR)]

            def one(i, _):
                for r in range(2):
                    grads = []
                    for v in range(NVAR):
                        a = f[i, c, r, v].astype(F32)
                        prev = hr[0, c, i, v].astype(F32)
                        nxt = hr[1, c, i, v].astype(F32)
                        if r == 0:
                            prev = pltpu.roll(prev, 4, 0)
                        else:
                            nxt = pltpu.roll(nxt, 4, 0)
                        total = None
                        for s in range(1, 4):
                            up = pltpu.roll(jnp.where(row >= s, a, nxt), 8 - s, 0)
                            down = pltpu.roll(jnp.where(row < 8 - s, a, prev), s, 0)
                            right = pltpu.roll(a, 256 - s, 1)
                            left = pltpu.roll(a, s, 1)
                            piece = COEFFS[s - 1] * ((up - down) + (right - left))
                            total = piece if total is None else total + piece
                        grads.append(total)
                    for v in range(NVAR):
                        m = weights[v][0] * grads[0]
                        for u in range(1, NVAR):
                            m = m + weights[v][u] * grads[u]
                        m = m.astype(BF)
                        g[2 * c][z, i, r, v] = m[:, :128]
                        g[2 * c + 1][z, i, r, v] = m[:, 128:]
                return 0

            lax.fori_loop(0, 2, one, 0)

        shift = [hidx[j] & (NH - 1) for j in range(NBASE)]
        whole = [h // NT for h in shift]
        rest_of = [h % NT for h in shift]
        owner_y = [own[j] // NZ for j in range(NBASE)]
        owner_z = [own[j] % NZ for j in range(NBASE)]

        row1 = lax.broadcasted_iota(jnp.int32, (8, 128), 0)
        damp = jnp.zeros((8, 128), F32)
        for r in range(8):
            damp = jnp.where(row1 == r, -2.0 * flg[r].astype(F32), damp)

        def partial(q):
            c, half = q // 2, q % 2
            buf = g[q]

            def one(i, _):
                t = 2 * z + i
                k = y * NT + t
                freq = 0.1 * jnp.where(k < NH // 2, k, k - NH).astype(F32)
                pick = [(t + NT - b) % NT for b in rest_of]
                off = [(a + jnp.where(t < b, 1, 0)) % NY for a, b in zip(whole, rest_of)]
                hot = [[jnp.where(off[j] == o, 1.0, 0.0).astype(F32) for o in range(NY)] for j in range(NBASE)]
                for v in range(NVAR):
                    fre = f[i, c, 0, v, :, 128 * half : 128 * half + 128].astype(F32)
                    fim = f[i, c, 1, v, :, 128 * half : 128 * half + 128].astype(F32)
                    sums_re = [damp * fre - freq * fim] + [None] * NO
                    sums_im = [damp * fim + freq * fre] + [None] * NO
                    for j in range(NBASE):
                        mre = buf[pick[j] // 2, pick[j] % 2, 0, v].astype(F32)
                        mim = buf[pick[j] // 2, pick[j] % 2, 1, v].astype(F32)
                        bre = bb[half, j, 0, v].astype(F32)
                        bim = bb[half, j, 1, v].astype(F32)
                        tre = bre * mre - bim * mim
                        tim = bre * mim + bim * mre
                        for o in range(NY):
                            if sums_re[o] is None:
                                sums_re[o] = hot[j][o] * tre
                                sums_im[o] = hot[j][o] * tim
                            else:
                                sums_re[o] = sums_re[o] + hot[j][o] * tre
                                sums_im[o] = sums_im[o] + hot[j][o] * tim
                    acc[q, i, 0, v] = sums_re[0]
                    acc[q, i, 1, v] = sums_im[0]
                    for o in range(1, NY):
                        ps[q, o - 1, i, 0, v] = sums_re[o].astype(BF)
                        ps[q, o - 1, i, 1, v] = sums_im[o].astype(BF)
                return 0

            lax.fori_loop(0, 2, one, 0)
            for o in range(1, NY):
                part(q, o).start()

        def finish(q):
            c, half = q // 2, q % 2
            for o in range(1, NY):
                part(q, o).wait_recv()

            def one(i, _):
                for r in range(2):
                    for v in range(NVAR):
                        total = acc[q, i, r, v]
                        for o in range(1, NY):
                            total = total + pr[q, o - 1, i, r, v].astype(F32)
                        ob[i, c, r, v, :, 128 * half : 128 * half + 128] = total.astype(BF)
                return 0

            lax.fori_loop(0, 2, one, 0)
            if half == 1:
                out_copy(c).start()

        for c in range(NCOL):
            halo(0, c).start()
            halo(1, c).start()
            if c == 0:
                ring(0, 0, 1).start()
                ring(0, 1, 1).start()

        done_p, done_f, ready_p, mixed_c = 0, 0, [], 0
        lag = 2
        p_tick = {}
        tick = 0
        base_tick = HA
        while done_f < CHUNKS:
            tick += 1
            for k in range(RING):
                hop = tick - inject[k]
                if 1 <= hop <= HA:
                    ring_arrived(k, 0, hop)
                    if hop < HA:
                        ring(k, 0, hop + 1).start()
                if 1 <= hop <= HB:
                    ring_arrived(k, 1, hop)
                    if hop < HB:
                        ring(k, 1, hop + 1).start()
            for k in range(1, RING):
                if inject[k] == tick:
                    c = (k - 1) // 2
                    if c >= mixed_c:
                        halo(0, c).wait_recv()
                        halo(1, c).wait_recv()
                        mixed(c)
                        mixed_c = c + 1
                    ring(k, 0, 1).start()
                    ring(k, 1, 1).start()
            if tick == base_tick:
                for j in range(NBASE):
                    for r in range(2):
                        for v in range(NVAR):
                            qr[y, j, r, v] = gb[owner_z[j], w, r, v]
                for o in range(1, NY):
                    base_row(o).start()
            if tick == base_tick + 1:
                for o in range(1, NY):
                    base_row_arrived(o)
                for j in range(NBASE):
                    for r in range(2):
                        for v in range(NVAR):
                            bb[w, j, r, v] = qr[owner_y[j], j, r, v]
                base_pair(w).start()
            if tick == base_tick + 2:
                base_pair(1 - w).wait_recv()
            if tick >= base_tick + 2:
                while done_p < CHUNKS and inject[done_p + 1] + HA <= tick:
                    partial(done_p)
                    p_tick[done_p] = tick
                    done_p += 1
            while done_f < done_p and (p_tick[done_f] + lag <= tick or done_p == CHUNKS):
                finish(done_f)
                done_f += 1

        for c in range(NCOL):
            halo(0, c).wait_send()
            halo(1, c).wait_send()
        for k in range(RING):
            for hop in range(1, HA + 1):
                ring(k, 0, hop).wait_send()
            for hop in range(1, HB + 1):
                ring(k, 1, hop).wait_send()
        for o in range(1, NY):
            base_row(o).wait_send()
        base_pair(w).wait_send()
        for q in range(CHUNKS):
            for o in range(1, NY):
                part(q, o).wait_send()
        for c in range(NCOL):
            out_copy(c).wait()

    block = (2, 2, NVAR, 8, 128)
    dma = pltpu.SemaphoreType.DMA
    scratch = [
        pltpu.VMEM((2, NCOL, 2, NVAR, 8, 256), BF),
        pltpu.VMEM((2, NVAR, 8, 256), BF),
        pltpu.VMEM((2, NCOL, 2, NVAR, 8, 256), BF),
        pltpu.VMEM((2, NCOL, 2, NVAR, 8, 256), BF),
        pltpu.VMEM((NZ, 2, 2, NVAR, 8, 128), BF),
        pltpu.VMEM((NY, NBASE, 2, NVAR, 8, 128), BF),
        pltpu.VMEM((2, NBASE, 2, NVAR, 8, 128), BF),
    ]
    scratch += [pltpu.VMEM((NZ,) + block, BF) for _ in range(CHUNKS)]
    scratch += [
        pltpu.VMEM((CHUNKS, NO) + block, BF),
        pltpu.VMEM((CHUNKS, NO) + block, BF),
        pltpu.VMEM((CHUNKS,) + block, F32),
        pltpu.VMEM((2, NCOL, 2, NVAR, 8, 256), BF),
        dma((NCOL + 1,)),
        dma((2, NCOL)), dma((2, NCOL)),
        dma((RING, HA)), dma((RING, HA)),
        dma((RING, HB)), dma((RING, HB)),
        dma((NO,)), dma((NO,)),
        dma((1,)), dma((1,)),
        dma((CHUNKS, NO)), dma((CHUNKS, NO)),
        dma((NCOL,)),
    ]
    smem = pl.BlockSpec(memory_space=pltpu.SMEM)
    hbm = pl.BlockSpec(memory_space=pl.ANY)

    def call(fields, base_store, harmonic_index, owners, sponge_flags, mixing):
        return pl.pallas_call(
            kernel,
            out_shape=jax.ShapeDtypeStruct(fields.shape, BF),
            in_specs=[hbm, hbm, smem, smem, smem, smem],
            out_specs=hbm,
            scratch_shapes=scratch,
            compiler_params=pltpu.CompilerParams(collective_id=0, has_side_effects=True),
            name="resolvent",
            interpret=interpret,
        )(fields, base_store, harmonic_index, owners, sponge_flags, mixing)

    return call


def wrap(mesh, call):
    return jax.shard_map(
        call,
        mesh=mesh,
        in_specs=(
            P("harm", None, None, None, "slab", None),
            P("harm", None, None, "slab", None),
            P(),
            P(),
            P("slab"),
            P(),
        ),
        out_specs=P("harm", None, None, None, "slab", None),
        check_vma=False,
    )


def solution(mesh):
    return wrap(mesh, build(4, mesh.shape["harm"] // 4, mesh.shape["slab"]))
```

```python
import jax
import jax.numpy as jnp
from jax import lax
from jax.experimental import pallas as pl
from jax.experimental.pallas import tpu as pltpu
from jax.sharding import PartitionSpec as P

COEFFS = (0.75, -0.15, 1.0 / 60.0)
NBASE = 3
NCOL = 4
NVAR = 5
CHUNKS = 8
MESH = pl.DeviceIdType.MESH
BF = jnp.bfloat16
F32 = jnp.float32


def build(NY, NZ, NS, interpret=False):
    NT = 2 * NZ
    NH = NY * NT
    HA = NZ // 2
    HB = NZ // 2 - 1
    NO = NY - 1
    ZSET = (0, 1, 4, 5)
    YSET = (2, 3, 6, 7)

    def kernel(f_hbm, b_hbm, hidx, own, flg, mix, o_hbm, f, bown, hs, hr, gb, qr, bb, *rest):
        g = rest[:CHUNKS]
        (ps, pr, acc, ob, ld_sem, h_send, h_recv, a_send, a_recv, b_send, b_recv, y_send, y_recv,
         x_send, x_recv, p_send, p_recv, o_sem, prod, cz, ra, rb, ra_send, ra_recv, rb_send, rb_recv) = rest[CHUNKS:]
        me = lax.axis_index("harm")
        slab = lax.axis_index("slab")
        y, z = me // NZ, me % NZ
        zside = (y * NZ + (z + 1) % NZ, y * NZ + (z + NZ - 1) % NZ)
        yside = [((y + o) % NY) * NZ + z for o in range(1, NY)]
        sside = ((slab + 1) % NS, (slab + NS - 1) % NS)

        loads = [pltpu.make_async_copy(b_hbm.at[0], bown, ld_sem.at[NCOL])]
        loads += [pltpu.make_async_copy(f_hbm.at[:, c], f.at[:, c], ld_sem.at[c]) for c in range(NCOL)]
        for load in loads:
            load.start()

        barrier = pltpu.get_barrier_semaphore()
        for n in zside:
            pl.semaphore_signal(barrier, inc=1, device_id={"harm": n}, device_id_type=MESH)
        for n in yside:
            pl.semaphore_signal(barrier, inc=1, device_id={"harm": n}, device_id_type=MESH)
        for n in sside:
            pl.semaphore_signal(barrier, inc=1, device_id={"slab": n}, device_id_type=MESH)

        row = lax.broadcasted_iota(jnp.int32, (8, 256), 0)

        def pack(c):
            def one(i, _):
                for v in range(NVAR):
                    re = f[i, c, 0, v].astype(F32)
                    im = f[i, c, 1, v].astype(F32)
                    hs[0, c, i, v] = jnp.where(row < 4, pltpu.roll(re, 4, 0), im).astype(BF)
                    hs[1, c, i, v] = jnp.where(row < 4, re, pltpu.roll(im, 4, 0)).astype(BF)
                return 0

            lax.fori_loop(0, 2, one, 0)

        loads[0].wait()
        for half in range(2):
            for r in range(2):
                for v in range(NVAR):
                    gb[z, half, r, v] = bown[r, v, :, 128 * half : 128 * half + 128]
        for c in range(NCOL):
            loads[1 + c].wait()
            pack(c)

        pl.semaphore_wait(barrier, 2 + NO + 2)

        def halo(d, c):
            return pltpu.make_async_remote_copy(
                hs.at[d, c], hr.at[d, c], h_send.at[d, c], h_recv.at[d, c],
                device_id={"slab": sside[d]}, device_id_type=MESH)

        def ring(k, way, hop):
            sign = 1 if (k + way) % 2 == 0 else -1
            origin = (z + NZ - sign * (hop - 1)) % NZ
            buf = gb if k == 0 else g[k - 1]
            send, recv = (a_send, a_recv) if way == 0 else (b_send, b_recv)
            return pltpu.make_async_remote_copy(
                buf.at[origin], buf.at[origin], send.at[k, hop - 1], recv.at[k, hop - 1],
                device_id={"harm": zside[0 if sign == 1 else 1]}, device_id_type=MESH)

        def ring_arrived(k, way, hop):
            sign = 1 if (k + way) % 2 == 0 else -1
            origin = (z + NZ - sign * hop) % NZ
            buf = gb if k == 0 else g[k - 1]
            send, recv = (a_send, a_recv) if way == 0 else (b_send, b_recv)
            pltpu.make_async_remote_copy(
                buf.at[origin], buf.at[origin], send.at[k, hop - 1], recv.at[k, hop - 1],
                device_id={"harm": zside[0 if sign == 1 else 1]}, device_id_type=MESH).wait_recv()

        def base_row(o):
            return pltpu.make_async_remote_copy(
                qr.at[y], qr.at[y], y_send.at[o - 1], y_recv.at[o - 1],
                device_id={"harm": yside[o - 1]}, device_id_type=MESH)

        def base_row_arrived(o):
            src = (y + NY - o) % NY
            pltpu.make_async_remote_copy(
                qr.at[src], qr.at[src], y_send.at[o - 1], y_recv.at[o - 1],
                device_id={"harm": yside[o - 1]}, device_id_type=MESH).wait_recv()

        w = z % 2
        pair = y * NZ + z + 1 - 2 * w

        def base_pair(slot):
            return pltpu.make_async_remote_copy(
                bb.at[slot], bb.at[slot], x_send.at[0], x_recv.at[0],
                device_id={"harm": pair}, device_id_type=MESH)

        def part(q, o):
            return pltpu.make_async_remote_copy(
                ps.at[q, o - 1], pr.at[q, o - 1], p_send.at[q, o - 1], p_recv.at[q, o - 1],
                device_id={"harm": yside[o - 1]}, device_id_type=MESH)

        def gather_row(q, o):
            return pltpu.make_async_remote_copy(
                g[q].at[y], g[q].at[y], p_send.at[q, o - 1], p_recv.at[q, o - 1],
                device_id={"harm": yside[o - 1]}, device_id_type=MESH)

        def gather_row_arrived(q, o):
            src = (y + NY - o) % NY
            pltpu.make_async_remote_copy(
                g[q].at[src], g[q].at[src], p_send.at[q, o - 1], p_recv.at[q, o - 1],
                device_id={"harm": yside[o - 1]}, device_id_type=MESH).wait_recv()

        def ring_sum(q, way, hop):
            n = YSET.index(q)
            sign = 1 if (q + way) % 2 == 0 else -1
            buf, send, recv, hops = (ra, ra_send, ra_recv, HA) if way == 0 else (rb, rb_send, rb_recv, HB)
            away = (sign * (hops + 1 - hop)) % NZ
            src = cz.at[n, away - 1] if hop == 1 else buf.at[n, hop - 2]
            return pltpu.make_async_remote_copy(
                src, buf.at[n, hop - 1], send.at[n, hop - 1], recv.at[n, hop - 1],
                device_id={"harm": zside[0 if sign == 1 else 1]}, device_id_type=MESH)

        def ring_sum_step(q, way, hop):
            n = YSET.index(q)
            sign = 1 if (q + way) % 2 == 0 else -1
            buf, hops = (ra, HA) if way == 0 else (rb, HB)
            away = (sign * (hops + 1 - hop)) % NZ
            ring_sum(q, way, hop - 1).wait_recv()

            def one(i, _):
                for r in range(2):
                    for v in range(NVAR):
                        buf[n, hop - 2, i, r, v] = (
                            buf[n, hop - 2, i, r, v].astype(F32) + cz[n, away - 1, i, r, v].astype(F32)
                        ).astype(BF)
                return 0

            lax.fori_loop(0, 2, one, 0)
            ring_sum(q, way, hop).start()

        def out_copy(c):
            return pltpu.make_async_copy(ob.at[:, c], o_hbm.at[:, c], o_sem.at[c])

        def mixed(c):
            weights = [[mix[v, u] for u in range(NVAR)] for v in range(NVAR)]
            slot = z if 2 * c in ZSET else y

            def one(i, _):
                for r in range(2):
                    grads = []
                    for v in range(NVAR):
                        a = f[i, c, r, v].astype(F32)
                        prev = hr[0, c, i, v].astype(F32)
                        nxt = hr[1, c, i, v].astype(F32)
                        if r == 0:
                            prev = pltpu.roll(prev, 4, 0)
                        else:
                            nxt = pltpu.roll(nxt, 4, 0)
                        total = None
                        for s in range(1, 4):
                            up = pltpu.roll(jnp.where(row >= s, a, nxt), 8 - s, 0)
                            down = pltpu.roll(jnp.where(row < 8 - s, a, prev), s, 0)
                            right = pltpu.roll(a, 256 - s, 1)
                            left = pltpu.roll(a, s, 1)
                            piece = COEFFS[s - 1] * ((up - down) + (right - left))
                            total = piece if total is None else total + piece
                        grads.append(total)
                    for v in range(NVAR):
                        m = weights[v][0] * grads[0]
                        for u in range(1, NVAR):
                            m = m + weights[v][u] * grads[u]
                        m = m.astype(BF)
                        g[2 * c][slot, i, r, v] = m[:, :128]
                        g[2 * c + 1][slot, i, r, v] = m[:, 128:]
                return 0

            lax.fori_loop(0, 2, one, 0)

        shift = [hidx[j] & (NH - 1) for j in range(NBASE)]
        whole = [h // NT for h in shift]
        rest_of = [h % NT for h in shift]
        owner_y = [own[j] // NZ for j in range(NBASE)]
        owner_z = [own[j] % NZ for j in range(NBASE)]

        row1 = lax.broadcasted_iota(jnp.int32, (8, 128), 0)
        damp = jnp.zeros((8, 128), F32)
        for r in range(8):
            damp = jnp.where(row1 == r, -2.0 * flg[r].astype(F32), damp)

        def partial(q):
            c, half = q // 2, q % 2
            buf = g[q]

            def one(i, _):
                t = 2 * z + i
                k = y * NT + t
                freq = 0.1 * jnp.where(k < NH // 2, k, k - NH).astype(F32)
                pick = [(t + NT - b) % NT for b in rest_of]
                off = [(a + jnp.where(t < b, 1, 0)) % NY for a, b in zip(whole, rest_of)]
                hot = [[jnp.where(off[j] == o, 1.0, 0.0).astype(F32) for o in range(NY)] for j in range(NBASE)]
                for v in range(NVAR):
                    fre = f[i, c, 0, v, :, 128 * half : 128 * half + 128].astype(F32)
                    fim = f[i, c, 1, v, :, 128 * half : 128 * half + 128].astype(F32)
                    sums_re = [damp * fre - freq * fim] + [None] * NO
                    sums_im = [damp * fim + freq * fre] + [None] * NO
                    for j in range(NBASE):
                        mre = buf[pick[j] // 2, pick[j] % 2, 0, v].astype(F32)
                        mim = buf[pick[j] // 2, pick[j] % 2, 1, v].astype(F32)
                        bre = bb[half, j, 0, v].astype(F32)
                        bim = bb[half, j, 1, v].astype(F32)
                        tre = bre * mre - bim * mim
                        tim = bre * mim + bim * mre
                        for o in range(NY):
                            if sums_re[o] is None:
                                sums_re[o] = hot[j][o] * tre
                                sums_im[o] = hot[j][o] * tim
                            else:
                                sums_re[o] = sums_re[o] + hot[j][o] * tre
                                sums_im[o] = sums_im[o] + hot[j][o] * tim
                    acc[q, i, 0, v] = sums_re[0]
                    acc[q, i, 1, v] = sums_im[0]
                    for o in range(1, NY):
                        ps[q, o - 1, i, 0, v] = sums_re[o].astype(BF)
                        ps[q, o - 1, i, 1, v] = sums_im[o].astype(BF)
                return 0

            lax.fori_loop(0, 2, one, 0)
            for o in range(1, NY):
                part(q, o).start()

        def shares(q):
            c, half = q // 2, q % 2
            n = YSET.index(q)
            buf = g[q]
            for o in range(1, NY):
                gather_row_arrived(q, o)

            def products(i, _):
                for j in range(NBASE):
                    t = (2 * z + i + rest_of[j]) % NT
                    src = (y + 2 * NY - whole[j] - jnp.where(t < rest_of[j], 1, 0)) % NY
                    for v in range(NVAR):
                        mre = buf[src, i, 0, v].astype(F32)
                        mim = buf[src, i, 1, v].astype(F32)
                        bre = bb[half, j, 0, v].astype(F32)
                        bim = bb[half, j, 1, v].astype(F32)
                        prod[j, i, 0, v] = bre * mre - bim * mim
                        prod[j, i, 1, v] = bre * mim + bim * mre
                return 0

            lax.fori_loop(0, 2, products, 0)

            def taken(away, i):
                t = 2 * ((z + away) % NZ) + i
                out = []
                for j in range(NBASE):
                    u = (t + NT - rest_of[j]) % NT
                    out.append(jnp.where(u // 2 == z, u % 2, 2))
                return out

            def one(e, _):
                away, i = e // 2, e % 2
                idx = taken(away, i)
                for r in range(2):
                    for v in range(NVAR):
                        total = prod[0, idx[0], r, v] + prod[1, idx[1], r, v] + prod[2, idx[2], r, v]
                        cz[n, away - 1, i, r, v] = total.astype(BF)
                return 0

            lax.fori_loop(2, 2 * NZ, one, 0)
            ring_sum(q, 0, 1).start()
            if HB:
                ring_sum(q, 1, 1).start()

            def here(i, _):
                idx = taken(0, i)
                k = y * NT + 2 * z + i
                freq = 0.1 * jnp.where(k < NH // 2, k, k - NH).astype(F32)
                for v in range(NVAR):
                    fre = f[i, c, 0, v, :, 128 * half : 128 * half + 128].astype(F32)
                    fim = f[i, c, 1, v, :, 128 * half : 128 * half + 128].astype(F32)
                    own_part = (damp * fre - freq * fim, damp * fim + freq * fre)
                    for r in range(2):
                        total = prod[0, idx[0], r, v] + prod[1, idx[1], r, v] + prod[2, idx[2], r, v]
                        acc[q, i, r, v] = own_part[r] + total
                return 0

            lax.fori_loop(0, 2, here, 0)

        def finish(q):
            c, half = q // 2, q % 2
            if q in ZSET:
                for o in range(1, NY):
                    part(q, o).wait_recv()
            else:
                ring_sum(q, 0, HA).wait_recv()
                ring_sum(q, 1, HB).wait_recv()

            def one(i, _):
                for r in range(2):
                    for v in range(NVAR):
                        total = acc[q, i, r, v]
                        if q in ZSET:
                            for o in range(1, NY):
                                total = total + pr[q, o - 1, i, r, v].astype(F32)
                        else:
                            n = YSET.index(q)
                            total = total + ra[n, HA - 1, i, r, v].astype(F32)
                            total = total + rb[n, HB - 1, i, r, v].astype(F32)
                        ob[i, c, r, v, :, 128 * half : 128 * half + 128] = total.astype(BF)
                return 0

            lax.fori_loop(0, 2, one, 0)
            if half == 1:
                out_copy(c).start()

        zero = jnp.zeros((8, 128), F32)
        for j in range(NBASE):
            for r in range(2):
                for v in range(NVAR):
                    prod[j, 2, r, v] = zero

        for c in range(NCOL):
            halo(0, c).start()
            halo(1, c).start()
            if c == 0:
                ring(0, 0, 1).start()
                ring(0, 1, 1).start()

        def relay(k, hop):
            if 1 <= hop <= HA:
                ring_arrived(k, 0, hop)
                if hop < HA:
                    ring(k, 0, hop + 1).start()
            if 1 <= hop <= HB:
                ring_arrived(k, 1, hop)
                if hop < HB:
                    ring(k, 1, hop + 1).start()

        def base_select():
            for j in range(NBASE):
                for r in range(2):
                    for v in range(NVAR):
                        qr[y, j, r, v] = gb[owner_z[j], w, r, v]
            for o in range(1, NY):
                base_row(o).start()

        def base_swap():
            for o in range(1, NY):
                base_row_arrived(o)
            for j in range(NBASE):
                for r in range(2):
                    for v in range(NVAR):
                        bb[w, j, r, v] = qr[owner_y[j], j, r, v]
            base_pair(w).start()

        for c in range(NCOL):
            if c % 2 == 0:
                relay(0, c // 2 + 1)
            halo(0, c).wait_recv()
            halo(1, c).wait_recv()
            mixed(c)
            for q in (2 * c, 2 * c + 1):
                if q in ZSET:
                    ring(q + 1, 0, 1).start()
                    ring(q + 1, 1, 1).start()
                else:
                    for o in range(1, NY):
                        gather_row(q, o).start()
        for hop in range(3, HA + 1):
            relay(0, hop)
            if hop < HA:
                for q in ZSET:
                    relay(q + 1, hop - 2)
        base_select()
        rest_hops = list(range(max(1, HA - 2), HA))
        for q in ZSET:
            relay(q + 1, rest_hops[0])
        base_swap()
        for hop in rest_hops[1:]:
            for q in ZSET:
                relay(q + 1, hop)
        base_pair(1 - w).wait_recv()
        for n in range(2):
            for q in YSET[2 * n : 2 * n + 2]:
                shares(q)
            for q in ZSET[2 * n : 2 * n + 2]:
                relay(q + 1, HA)
                partial(q)
        for hop in range(2, HA + 1):
            for q in YSET:
                ring_sum_step(q, 0, hop)
                if hop <= HB:
                    ring_sum_step(q, 1, hop)
        for q in range(CHUNKS):
            finish(q)

        for c in range(NCOL):
            halo(0, c).wait_send()
            halo(1, c).wait_send()
        for k in (0,) + tuple(q + 1 for q in ZSET):
            for hop in range(1, HA + 1):
                ring(k, 0, hop).wait_send()
            for hop in range(1, HB + 1):
                ring(k, 1, hop).wait_send()
        for o in range(1, NY):
            base_row(o).wait_send()
        base_pair(w).wait_send()
        for q in ZSET:
            for o in range(1, NY):
                part(q, o).wait_send()
        for q in YSET:
            for o in range(1, NY):
                gather_row(q, o).wait_send()
            for hop in range(1, HA + 1):
                ring_sum(q, 0, hop).wait_send()
            for hop in range(1, HB + 1):
                ring_sum(q, 1, hop).wait_send()
        for c in range(NCOL):
            out_copy(c).wait()

    block = (2, 2, NVAR, 8, 128)
    dma = pltpu.SemaphoreType.DMA
    scratch = [
        pltpu.VMEM((2, NCOL, 2, NVAR, 8, 256), BF),
        pltpu.VMEM((2, NVAR, 8, 256), BF),
        pltpu.VMEM((2, NCOL, 2, NVAR, 8, 256), BF),
        pltpu.VMEM((2, NCOL, 2, NVAR, 8, 256), BF),
        pltpu.VMEM((NZ, 2, 2, NVAR, 8, 128), BF),
        pltpu.VMEM((NY, NBASE, 2, NVAR, 8, 128), BF),
        pltpu.VMEM((2, NBASE, 2, NVAR, 8, 128), BF),
    ]
    scratch += [pltpu.VMEM((NZ if q in ZSET else NY,) + block, BF) for q in range(CHUNKS)]
    scratch += [
        pltpu.VMEM((CHUNKS, NO) + block, BF),
        pltpu.VMEM((CHUNKS, NO) + block, BF),
        pltpu.VMEM((CHUNKS,) + block, F32),
        pltpu.VMEM((2, NCOL, 2, NVAR, 8, 256), BF),
        dma((NCOL + 1,)),
        dma((2, NCOL)), dma((2, NCOL)),
        dma((CHUNKS + 1, HA)), dma((CHUNKS + 1, HA)),
        dma((CHUNKS + 1, HB)), dma((CHUNKS + 1, HB)),
        dma((NO,)), dma((NO,)),
        dma((1,)), dma((1,)),
        dma((CHUNKS, NO)), dma((CHUNKS, NO)),
        dma((NCOL,)),
        pltpu.VMEM((NBASE, 3, 2, NVAR, 8, 128), F32),
        pltpu.VMEM((len(YSET), NZ - 1) + block, BF),
        pltpu.VMEM((len(YSET), HA) + block, BF),
        pltpu.VMEM((len(YSET), HB) + block, BF),
        dma((len(YSET), HA)), dma((len(YSET), HA)),
        dma((len(YSET), HB)), dma((len(YSET), HB)),
    ]
    smem = pl.BlockSpec(memory_space=pltpu.SMEM)
    hbm = pl.BlockSpec(memory_space=pl.ANY)

    def call(fields, base_store, harmonic_index, owners, sponge_flags, mixing):
        return pl.pallas_call(
            kernel,
            out_shape=jax.ShapeDtypeStruct(fields.shape, BF),
            in_specs=[hbm, hbm, smem, smem, smem, smem],
            out_specs=hbm,
            scratch_shapes=scratch,
            compiler_params=pltpu.CompilerParams(collective_id=0, has_side_effects=True),
            name="resolvent",
            interpret=interpret,
        )(fields, base_store, harmonic_index, owners, sponge_flags, mixing)

    return call


def wrap(mesh, call):
    return jax.shard_map(
        call,
        mesh=mesh,
        in_specs=(
            P("harm", None, None, None, "slab", None),
            P("harm", None, None, "slab", None),
            P(),
            P(),
            P("slab"),
            P(),
        ),
        out_specs=P("harm", None, None, None, "slab", None),
        check_vma=False,
    )


def solution(mesh):
    return wrap(mesh, build(4, mesh.shape["harm"] // 4, mesh.shape["slab"]))
```

```python
import jax
import jax.numpy as jnp
from jax import lax
from jax.experimental import pallas as pl
from jax.experimental.pallas import tpu as pltpu
from jax.sharding import PartitionSpec as P

COEFFS = (0.75, -0.15, 1.0 / 60.0)
NBASE = 3
NCOL = 4
NVAR = 5
CHUNKS = 8
COLLECT = 13
SPREAD = 5
MESH = pl.DeviceIdType.MESH
BF = jnp.bfloat16
F32 = jnp.float32


def build(NY, NZ, NS, interpret=False):
    NT = 2 * NZ
    NH = NY * NT
    HA = NZ // 2
    HB = NZ // 2 - 1
    NO = NY - 1
    G = NY * NZ
    TILES = 4 * NVAR
    ROUNDS = -(-TILES // G)
    FORWARD = NY == 4
    ZSET = (0, 1, 4, 5)
    YSET = (2, 3, 6, 7)

    def kernel(f_hbm, b_hbm, hidx, own, flg, mix, o_hbm, f, bown, bt, hs, hr, pa, pb, *rest):
        g = rest[:CHUNKS]
        (ps, pr, acc, ob, ld_sem, h_send, h_recv, a_send, a_recv, b_send, b_recv, t_send, t_recv, u_send, u_recv,
         p_send, p_recv, o_sem, prod, cz, ra, rb, ra_send, ra_recv, rb_send, rb_recv, f_send) = rest[CHUNKS:]
        me = lax.axis_index("harm")
        slab = lax.axis_index("slab")
        y, z = me // NZ, me % NZ
        zside = (y * NZ + (z + 1) % NZ, y * NZ + (z + NZ - 1) % NZ)
        yside = [((y + o) % NY) * NZ + z for o in range(1, NY)]
        sside = ((slab + 1) % NS, (slab + NS - 1) % NS)

        loads = [pltpu.make_async_copy(b_hbm, bown, ld_sem.at[NCOL])]
        loads += [pltpu.make_async_copy(f_hbm.at[:, c], f.at[:, c], ld_sem.at[c]) for c in range(NCOL)]
        for load in loads:
            load.start()

        def others(act):
            def one(o, _):
                act((me + o) % G)
                return 0

            lax.fori_loop(1, G, one, 0)

        barrier = pltpu.get_barrier_semaphore()
        others(lambda d: pl.semaphore_signal(barrier, inc=1, device_id={"harm": d}, device_id_type=MESH))
        for n in sside:
            pl.semaphore_signal(barrier, inc=1, device_id={"slab": n}, device_id_type=MESH)

        row = lax.broadcasted_iota(jnp.int32, (8, 256), 0)

        def pack(c):
            def one(i, _):
                for v in range(NVAR):
                    re = f[i, c, 0, v].astype(F32)
                    im = f[i, c, 1, v].astype(F32)
                    hs[0, c, i, v] = jnp.where(row < 4, pltpu.roll(re, 4, 0), im).astype(BF)
                    hs[1, c, i, v] = jnp.where(row < 4, re, pltpu.roll(im, 4, 0)).astype(BF)
                return 0

            lax.fori_loop(0, 2, one, 0)

        loads[0].wait()
        for half in range(2):
            for p in range(2 * NVAR):
                bt[2 * NVAR * half + p] = bown[p, :, 128 * half : 128 * half + 128]
        for c in range(NCOL):
            loads[1 + c].wait()
            pack(c)

        pl.semaphore_wait(barrier, G - 1 + 2)

        def halo(d, c):
            return pltpu.make_async_remote_copy(
                hs.at[d, c], hr.at[d, c], h_send.at[d, c], h_recv.at[d, c],
                device_id={"slab": sside[d]}, device_id_type=MESH)

        def ring(k, way, hop):
            sign = 1 if (k + way) % 2 == 0 else -1
            origin = (z + NZ - sign * (hop - 1)) % NZ
            buf = g[k]
            send, recv = (a_send, a_recv) if way == 0 else (b_send, b_recv)
            return pltpu.make_async_remote_copy(
                buf.at[origin], buf.at[origin], send.at[k, hop - 1], recv.at[k, hop - 1],
                device_id={"harm": zside[0 if sign == 1 else 1]}, device_id_type=MESH)

        def ring_arrived(k, way, hop):
            sign = 1 if (k + way) % 2 == 0 else -1
            origin = (z + NZ - sign * hop) % NZ
            buf = g[k]
            send, recv = (a_send, a_recv) if way == 0 else (b_send, b_recv)
            pltpu.make_async_remote_copy(
                buf.at[origin], buf.at[origin], send.at[k, hop - 1], recv.at[k, hop - 1],
                device_id={"harm": zside[0 if sign == 1 else 1]}, device_id_type=MESH).wait_recv()

        def tile_at(rnd):
            return SPREAD * me % G + rnd * G

        mine = sum(jnp.where(tile_at(rnd) < TILES, 1, 0) for rnd in range(ROUNDS))

        def tile_in(p):
            return pltpu.make_async_remote_copy(
                bt.at[p], pa.at[p // G, me], t_send.at[0], t_recv.at[p // G],
                device_id={"harm": COLLECT * p % G}, device_id_type=MESH)

        def tile_out(p, d, rnd):
            return pltpu.make_async_remote_copy(
                pb.at[p], pb.at[p], u_send.at[rnd, d], u_recv.at[0],
                device_id={"harm": d}, device_id_type=MESH)

        def bytes_of(ref, sem):
            pltpu.make_async_copy(ref, ref, sem).wait()

        def all_tiles(ref, sem):
            for n in range(ROUNDS + 1):
                pl.when(mine == n)(lambda n=n: bytes_of(ref.at[pl.ds(0, TILES - n)], sem))

        def tiles_start():
            for p in range(TILES):
                pl.when(COLLECT * p % G != me)(lambda p=p: tile_in(p).start())
            collected(keep)

        def collected(act):
            for rnd in range(ROUNDS):
                p = tile_at(rnd)
                pl.when(p < TILES)(lambda p=p, rnd=rnd: act(p, rnd))

        def collect(p, rnd):
            bytes_of(pa.at[rnd, pl.ds(0, G - 1)], t_recv.at[rnd])
            for j in range(NBASE):
                pb[p, j] = pa[rnd, own[j]]
            others(lambda d: tile_out(p, d, rnd).start())

        def keep(p, rnd):
            pa[rnd, me] = bt[p]

        def part(q, o):
            return pltpu.make_async_remote_copy(
                ps.at[q, o - 1], pr.at[q, o - 1], p_send.at[q, o - 1], p_recv.at[q, o - 1],
                device_id={"harm": yside[o - 1]}, device_id_type=MESH)

        def gather_row(q, o):
            return pltpu.make_async_remote_copy(
                g[q].at[y], g[q].at[y], p_send.at[q, o - 1], p_recv.at[q, o - 1],
                device_id={"harm": yside[o - 1]}, device_id_type=MESH)

        def gather_row_arrived(q, o):
            src = (y + NY - o) % NY
            pltpu.make_async_remote_copy(
                g[q].at[src], g[q].at[src], p_send.at[q, o - 1], p_recv.at[q, o - 1],
                device_id={"harm": yside[o - 1]}, device_id_type=MESH).wait_recv()

        middle = (y == 1) | (y == 2) if FORWARD else False

        def gather_row_each(act):
            for o in range(1, NY):
                if FORWARD and o != 2:
                    pl.when(y != (3 if o == 1 else 0))(lambda o=o: act(o))
                else:
                    act(o)

        def handed(q):
            src = (y + 2) % NY
            return pltpu.make_async_remote_copy(
                g[q].at[src], g[q].at[src], f_send.at[q], p_recv.at[q, 2 * (y - 1)],
                device_id={"harm": (3 * (y - 1)) * NZ + z}, device_id_type=MESH)

        def hand_on(q):
            if FORWARD:
                @pl.when(middle)
                def _():
                    gather_row_arrived(q, 2)
                    handed(q).start()

        def ring_sum(q, way, hop):
            n = YSET.index(q)
            sign = 1 if (q + way) % 2 == 0 else -1
            buf, send, recv, hops = (ra, ra_send, ra_recv, HA) if way == 0 else (rb, rb_send, rb_recv, HB)
            away = (sign * (hops + 1 - hop)) % NZ
            src = cz.at[n, away - 1] if hop == 1 else buf.at[n, hop - 2]
            return pltpu.make_async_remote_copy(
                src, buf.at[n, hop - 1], send.at[n, hop - 1], recv.at[n, hop - 1],
                device_id={"harm": zside[0 if sign == 1 else 1]}, device_id_type=MESH)

        def ring_sum_step(q, way, hop):
            n = YSET.index(q)
            sign = 1 if (q + way) % 2 == 0 else -1
            buf, hops = (ra, HA) if way == 0 else (rb, HB)
            away = (sign * (hops + 1 - hop)) % NZ
            ring_sum(q, way, hop - 1).wait_recv()

            def one(i, _):
                for r in range(2):
                    for v in range(NVAR):
                        buf[n, hop - 2, i, r, v] = (
                            buf[n, hop - 2, i, r, v].astype(F32) + cz[n, away - 1, i, r, v].astype(F32)
                        ).astype(BF)
                return 0

            lax.fori_loop(0, 2, one, 0)
            ring_sum(q, way, hop).start()

        def out_copy(c):
            return pltpu.make_async_copy(ob.at[:, c], o_hbm.at[:, c], o_sem.at[c])

        def mixed(c):
            weights = [[mix[v, u] for u in range(NVAR)] for v in range(NVAR)]
            slot = z if 2 * c in ZSET else y

            def one(i, _):
                for r in range(2):
                    grads = []
                    for v in range(NVAR):
                        a = f[i, c, r, v].astype(F32)
                        prev = hr[0, c, i, v].astype(F32)
                        nxt = hr[1, c, i, v].astype(F32)
                        if r == 0:
                            prev = pltpu.roll(prev, 4, 0)
                        else:
                            nxt = pltpu.roll(nxt, 4, 0)
                        total = None
                        for s in range(1, 4):
                            up = pltpu.roll(jnp.where(row >= s, a, nxt), 8 - s, 0)
                            down = pltpu.roll(jnp.where(row < 8 - s, a, prev), s, 0)
                            right = pltpu.roll(a, 256 - s, 1)
                            left = pltpu.roll(a, s, 1)
                            piece = COEFFS[s - 1] * ((up - down) + (right - left))
                            total = piece if total is None else total + piece
                        grads.append(total)
                    for v in range(NVAR):
                        m = weights[v][0] * grads[0]
                        for u in range(1, NVAR):
                            m = m + weights[v][u] * grads[u]
                        m = m.astype(BF)
                        g[2 * c][slot, i, r, v] = m[:, :128]
                        g[2 * c + 1][slot, i, r, v] = m[:, 128:]
                return 0

            lax.fori_loop(0, 2, one, 0)

        shift = [hidx[j] & (NH - 1) for j in range(NBASE)]
        whole = [h // NT for h in shift]
        rest_of = [h % NT for h in shift]

        row1 = lax.broadcasted_iota(jnp.int32, (8, 128), 0)
        damp = jnp.zeros((8, 128), F32)
        for r in range(8):
            damp = jnp.where(row1 == r, -2.0 * flg[r].astype(F32), damp)

        def partial(q):
            c, half = q // 2, q % 2
            buf = g[q]

            def one(i, _):
                t = 2 * z + i
                k = y * NT + t
                freq = 0.1 * jnp.where(k < NH // 2, k, k - NH).astype(F32)
                pick = [(t + NT - b) % NT for b in rest_of]
                off = [(a + jnp.where(t < b, 1, 0)) % NY for a, b in zip(whole, rest_of)]
                hot = [[jnp.where(off[j] == o, 1.0, 0.0).astype(F32) for o in range(NY)] for j in range(NBASE)]
                for v in range(NVAR):
                    fre = f[i, c, 0, v, :, 128 * half : 128 * half + 128].astype(F32)
                    fim = f[i, c, 1, v, :, 128 * half : 128 * half + 128].astype(F32)
                    sums_re = [damp * fre - freq * fim] + [None] * NO
                    sums_im = [damp * fim + freq * fre] + [None] * NO
                    for j in range(NBASE):
                        mre = buf[pick[j] // 2, pick[j] % 2, 0, v].astype(F32)
                        mim = buf[pick[j] // 2, pick[j] % 2, 1, v].astype(F32)
                        bre = pb[2 * half * NVAR + v, j].astype(F32)
                        bim = pb[(2 * half + 1) * NVAR + v, j].astype(F32)
                        tre = bre * mre - bim * mim
                        tim = bre * mim + bim * mre
                        for o in range(NY):
                            if sums_re[o] is None:
                                sums_re[o] = hot[j][o] * tre
                                sums_im[o] = hot[j][o] * tim
                            else:
                                sums_re[o] = sums_re[o] + hot[j][o] * tre
                                sums_im[o] = sums_im[o] + hot[j][o] * tim
                    acc[q, i, 0, v] = sums_re[0]
                    acc[q, i, 1, v] = sums_im[0]
                    for o in range(1, NY):
                        ps[q, o - 1, i, 0, v] = sums_re[o].astype(BF)
                        ps[q, o - 1, i, 1, v] = sums_im[o].astype(BF)
                return 0

            lax.fori_loop(0, 2, one, 0)
            for o in range(1, NY):
                part(q, o).start()

        def shares(q):
            c, half = q // 2, q % 2
            n = YSET.index(q)
            buf = g[q]
            for o in range(1, NY):
                if FORWARD and o == 2:
                    pl.when(jnp.logical_not(middle))(lambda: gather_row_arrived(q, 2))
                else:
                    gather_row_arrived(q, o)

            def products(i, _):
                for j in range(NBASE):
                    t = (2 * z + i + rest_of[j]) % NT
                    src = (y + 2 * NY - whole[j] - jnp.where(t < rest_of[j], 1, 0)) % NY
                    for v in range(NVAR):
                        mre = buf[src, i, 0, v].astype(F32)
                        mim = buf[src, i, 1, v].astype(F32)
                        bre = pb[2 * half * NVAR + v, j].astype(F32)
                        bim = pb[(2 * half + 1) * NVAR + v, j].astype(F32)
                        prod[j, i, 0, v] = bre * mre - bim * mim
                        prod[j, i, 1, v] = bre * mim + bim * mre
                return 0

            lax.fori_loop(0, 2, products, 0)

            def taken(away, i):
                t = 2 * ((z + away) % NZ) + i
                out = []
                for j in range(NBASE):
                    u = (t + NT - rest_of[j]) % NT
                    out.append(jnp.where(u // 2 == z, u % 2, 2))
                return out

            def one(e, _):
                away, i = e // 2, e % 2
                idx = taken(away, i)
                for r in range(2):
                    for v in range(NVAR):
                        total = prod[0, idx[0], r, v] + prod[1, idx[1], r, v] + prod[2, idx[2], r, v]
                        cz[n, away - 1, i, r, v] = total.astype(BF)
                return 0

            lax.fori_loop(2, 2 * NZ, one, 0)
            ring_sum(q, 0, 1).start()
            if HB:
                ring_sum(q, 1, 1).start()

            def here(i, _):
                idx = taken(0, i)
                k = y * NT + 2 * z + i
                freq = 0.1 * jnp.where(k < NH // 2, k, k - NH).astype(F32)
                for v in range(NVAR):
                    fre = f[i, c, 0, v, :, 128 * half : 128 * half + 128].astype(F32)
                    fim = f[i, c, 1, v, :, 128 * half : 128 * half + 128].astype(F32)
                    own_part = (damp * fre - freq * fim, damp * fim + freq * fre)
                    for r in range(2):
                        total = prod[0, idx[0], r, v] + prod[1, idx[1], r, v] + prod[2, idx[2], r, v]
                        acc[q, i, r, v] = own_part[r] + total
                return 0

            lax.fori_loop(0, 2, here, 0)

        def finish(q):
            c, half = q // 2, q % 2
            if q in ZSET:
                for o in range(1, NY):
                    part(q, o).wait_recv()
            else:
                ring_sum(q, 0, HA).wait_recv()
                ring_sum(q, 1, HB).wait_recv()

            def one(i, _):
                for r in range(2):
                    for v in range(NVAR):
                        total = acc[q, i, r, v]
                        if q in ZSET:
                            for o in range(1, NY):
                                total = total + pr[q, o - 1, i, r, v].astype(F32)
                        else:
                            n = YSET.index(q)
                            total = total + ra[n, HA - 1, i, r, v].astype(F32)
                            total = total + rb[n, HB - 1, i, r, v].astype(F32)
                        ob[i, c, r, v, :, 128 * half : 128 * half + 128] = total.astype(BF)
                return 0

            lax.fori_loop(0, 2, one, 0)
            if half == 1:
                out_copy(c).start()

        zero = jnp.zeros((8, 128), F32)
        for j in range(NBASE):
            for r in range(2):
                for v in range(NVAR):
                    prod[j, 2, r, v] = zero

        for c in range(NCOL):
            halo(0, c).start()
            halo(1, c).start()
            if c == 0:
                tiles_start()

        def relay(q, hop):
            if 1 <= hop <= HA:
                ring_arrived(q, 0, hop)
                if hop < HA:
                    ring(q, 0, hop + 1).start()
            if 1 <= hop <= HB:
                ring_arrived(q, 1, hop)
                if hop < HB:
                    ring(q, 1, hop + 1).start()

        for c in range(NCOL):
            halo(0, c).wait_recv()
            halo(1, c).wait_recv()
            mixed(c)
            for q in (2 * c, 2 * c + 1):
                if q in ZSET:
                    ring(q, 0, 1).start()
                    ring(q, 1, 1).start()
                else:
                    gather_row_each(lambda o, q=q: gather_row(q, o).start())
        for hop in range(1, HA):
            for q in ZSET:
                relay(q, hop)
            if hop == 1:
                collected(collect)
                for q in YSET[:2]:
                    hand_on(q)
            if hop == 2:
                for q in YSET[2:]:
                    hand_on(q)
        all_tiles(pb, u_recv.at[0])
        for n in range(2):
            for q in YSET[2 * n : 2 * n + 2]:
                shares(q)
            for q in ZSET[2 * n : 2 * n + 2]:
                relay(q, HA)
                partial(q)
        for hop in range(2, HA + 1):
            for q in YSET:
                ring_sum_step(q, 0, hop)
                if hop <= HB:
                    ring_sum_step(q, 1, hop)
        for c in range(NCOL):
            halo(0, c).wait_send()
            halo(1, c).wait_send()
        for q in ZSET:
            for hop in range(1, HA + 1):
                ring(q, 0, hop).wait_send()
            for hop in range(1, HB + 1):
                ring(q, 1, hop).wait_send()
        all_tiles(bt, t_send.at[0])
        collected(lambda p, rnd: others(lambda d: tile_out(p, d, rnd).wait_send()))
        for q in YSET:
            gather_row_each(lambda o, q=q: gather_row(q, o).wait_send())
            if FORWARD:
                pl.when(middle)(lambda q=q: handed(q).wait_send())
            for hop in range(1, HA):
                ring_sum(q, 0, hop).wait_send()
                if hop < HB:
                    ring_sum(q, 1, hop).wait_send()
        for q in range(CHUNKS):
            finish(q)
        for q in ZSET:
            for o in range(1, NY):
                part(q, o).wait_send()
        for q in YSET:
            ring_sum(q, 0, HA).wait_send()
            ring_sum(q, 1, HB).wait_send()
        for c in range(NCOL):
            out_copy(c).wait()

    block = (2, 2, NVAR, 8, 128)
    dma = pltpu.SemaphoreType.DMA
    scratch = [
        pltpu.VMEM((2, NCOL, 2, NVAR, 8, 256), BF),
        pltpu.VMEM((2 * NVAR, 8, 256), BF),
        pltpu.VMEM((TILES, 8, 128), BF),
        pltpu.VMEM((2, NCOL, 2, NVAR, 8, 256), BF),
        pltpu.VMEM((2, NCOL, 2, NVAR, 8, 256), BF),
        pltpu.VMEM((ROUNDS, G, 8, 128), BF),
        pltpu.VMEM((TILES, NBASE, 8, 128), BF),
    ]
    scratch += [pltpu.VMEM((NZ if q in ZSET else NY,) + block, BF) for q in range(CHUNKS)]
    scratch += [
        pltpu.VMEM((CHUNKS, NO) + block, BF),
        pltpu.VMEM((CHUNKS, NO) + block, BF),
        pltpu.VMEM((CHUNKS,) + block, F32),
        pltpu.VMEM((2, NCOL, 2, NVAR, 8, 256), BF),
        dma((NCOL + 1,)),
        dma((2, NCOL)), dma((2, NCOL)),
        dma((CHUNKS, HA)), dma((CHUNKS, HA)),
        dma((CHUNKS, HB)), dma((CHUNKS, HB)),
        dma((1,)), dma((ROUNDS,)),
        dma((ROUNDS, G)), dma((1,)),
        dma((CHUNKS, NO)), dma((CHUNKS, NO)),
        dma((NCOL,)),
        pltpu.VMEM((NBASE, 3, 2, NVAR, 8, 128), F32),
        pltpu.VMEM((len(YSET), NZ - 1) + block, BF),
        pltpu.VMEM((len(YSET), HA) + block, BF),
        pltpu.VMEM((len(YSET), HB) + block, BF),
        dma((len(YSET), HA)), dma((len(YSET), HA)),
        dma((len(YSET), HB)), dma((len(YSET), HB)),
        dma((CHUNKS,)),
    ]
    smem = pl.BlockSpec(memory_space=pltpu.SMEM)
    hbm = pl.BlockSpec(memory_space=pl.ANY)

    def call(fields, base_store, harmonic_index, owners, sponge_flags, mixing):
        return pl.pallas_call(
            kernel,
            out_shape=jax.ShapeDtypeStruct(fields.shape, BF),
            in_specs=[hbm, hbm, smem, smem, smem, smem],
            out_specs=hbm,
            scratch_shapes=scratch,
            compiler_params=pltpu.CompilerParams(collective_id=0, has_side_effects=True),
            name="resolvent",
            interpret=interpret,
        )(fields, base_store.reshape(2 * NVAR, 8, 256), harmonic_index, owners, sponge_flags, mixing)

    return call


def wrap(mesh, call):
    return jax.shard_map(
        call,
        mesh=mesh,
        in_specs=(
            P("harm", None, None, None, "slab", None),
            P("harm", None, None, "slab", None),
            P(),
            P(),
            P("slab"),
            P(),
        ),
        out_specs=P("harm", None, None, None, "slab", None),
        check_vma=False,
    )


def solution(mesh):
    return wrap(mesh, build(4, mesh.shape["harm"] // 4, mesh.shape["slab"]))
```

```python
import jax
import jax.numpy as jnp
from jax import lax
from jax.experimental import pallas as pl
from jax.experimental.pallas import tpu as pltpu
from jax.sharding import PartitionSpec as P

COEFFS = (0.75, -0.15, 1.0 / 60.0)
NBASE = 3
NCOL = 4
NVAR = 5
CHUNKS = 8
COLLECT = 13
SPREAD = 5
MESH = pl.DeviceIdType.MESH
BF = jnp.bfloat16
F32 = jnp.float32


def build(NY, NZ, NS, interpret=False):
    NT = 2 * NZ
    NH = NY * NT
    HA = NZ // 2
    HB = NZ // 2 - 1
    NO = NY - 1
    G = NY * NZ
    TILES = 4 * NVAR
    ROUNDS = -(-TILES // G)
    FORWARD = NY == 4
    ZSET = (0, 1, 3, 4, 5)
    YSET = (2, 6, 7)

    def kernel(f_hbm, b_hbm, hidx, own, flg, mix, o_hbm, f, bown, bt, hs, hr, pa, pb, *rest):
        g = rest[:CHUNKS]
        (ps, pr, acc, ob, ld_sem, h_send, h_recv, a_send, a_recv, b_send, b_recv, t_send, t_recv, u_send, u_recv,
         p_send, p_recv, o_sem, prod, cz, ra, rb, ra_send, ra_recv, rb_send, rb_recv, f_send) = rest[CHUNKS:]
        me = lax.axis_index("harm")
        slab = lax.axis_index("slab")
        y, z = me // NZ, me % NZ
        zside = (y * NZ + (z + 1) % NZ, y * NZ + (z + NZ - 1) % NZ)
        yside = [((y + o) % NY) * NZ + z for o in range(1, NY)]
        sside = ((slab + 1) % NS, (slab + NS - 1) % NS)

        loads = [pltpu.make_async_copy(b_hbm, bown, ld_sem.at[NCOL])]
        loads += [pltpu.make_async_copy(f_hbm.at[:, c], f.at[:, c], ld_sem.at[c]) for c in range(NCOL)]
        for load in loads:
            load.start()

        def others(act):
            def one(o, _):
                act((me + o) % G)
                return 0

            lax.fori_loop(1, G, one, 0)

        barrier = pltpu.get_barrier_semaphore()
        others(lambda d: pl.semaphore_signal(barrier, inc=1, device_id={"harm": d}, device_id_type=MESH))
        for n in sside:
            pl.semaphore_signal(barrier, inc=1, device_id={"slab": n}, device_id_type=MESH)

        row = lax.broadcasted_iota(jnp.int32, (8, 256), 0)

        def pack(c):
            def one(i, _):
                for v in range(NVAR):
                    re = f[i, c, 0, v].astype(F32)
                    im = f[i, c, 1, v].astype(F32)
                    hs[0, c, i, v] = jnp.where(row < 4, pltpu.roll(re, 4, 0), im).astype(BF)
                    hs[1, c, i, v] = jnp.where(row < 4, re, pltpu.roll(im, 4, 0)).astype(BF)
                return 0

            lax.fori_loop(0, 2, one, 0)

        loads[0].wait()
        for half in range(2):
            for p in range(2 * NVAR):
                bt[2 * NVAR * half + p] = bown[p, :, 128 * half : 128 * half + 128]
        for c in range(NCOL):
            loads[1 + c].wait()
            pack(c)

        pl.semaphore_wait(barrier, G - 1 + 2)

        def halo(d, c):
            return pltpu.make_async_remote_copy(
                hs.at[d, c], hr.at[d, c], h_send.at[d, c], h_recv.at[d, c],
                device_id={"slab": sside[d]}, device_id_type=MESH)

        def ring(k, way, hop):
            sign = 1 if (k + way) % 2 == 0 else -1
            origin = (z + NZ - sign * (hop - 1)) % NZ
            buf = g[k]
            send, recv = (a_send, a_recv) if way == 0 else (b_send, b_recv)
            return pltpu.make_async_remote_copy(
                buf.at[origin], buf.at[origin], send.at[k, hop - 1], recv.at[k, hop - 1],
                device_id={"harm": zside[0 if sign == 1 else 1]}, device_id_type=MESH)

        def ring_arrived(k, way, hop):
            sign = 1 if (k + way) % 2 == 0 else -1
            origin = (z + NZ - sign * hop) % NZ
            buf = g[k]
            send, recv = (a_send, a_recv) if way == 0 else (b_send, b_recv)
            pltpu.make_async_remote_copy(
                buf.at[origin], buf.at[origin], send.at[k, hop - 1], recv.at[k, hop - 1],
                device_id={"harm": zside[0 if sign == 1 else 1]}, device_id_type=MESH).wait_recv()

        def tile_at(rnd):
            return SPREAD * me % G + rnd * G

        mine = sum(jnp.where(tile_at(rnd) < TILES, 1, 0) for rnd in range(ROUNDS))

        def tile_in(p):
            return pltpu.make_async_remote_copy(
                bt.at[p], pa.at[p // G, me], t_send.at[0], t_recv.at[p // G],
                device_id={"harm": COLLECT * p % G}, device_id_type=MESH)

        def tile_out(p, d, rnd):
            return pltpu.make_async_remote_copy(
                pb.at[p], pb.at[p], u_send.at[rnd, d], u_recv.at[0],
                device_id={"harm": d}, device_id_type=MESH)

        def bytes_of(ref, sem):
            pltpu.make_async_copy(ref, ref, sem).wait()

        def all_tiles(ref, sem):
            for n in range(ROUNDS + 1):
                pl.when(mine == n)(lambda n=n: bytes_of(ref.at[pl.ds(0, TILES - n)], sem))

        def tiles_start():
            for p in range(TILES):
                pl.when(COLLECT * p % G != me)(lambda p=p: tile_in(p).start())
            collected(keep)

        def collected(act):
            for rnd in range(ROUNDS):
                p = tile_at(rnd)
                pl.when(p < TILES)(lambda p=p, rnd=rnd: act(p, rnd))

        def collect(p, rnd):
            bytes_of(pa.at[rnd, pl.ds(0, G - 1)], t_recv.at[rnd])
            for j in range(NBASE):
                pb[p, j] = pa[rnd, own[j]]
            others(lambda d: tile_out(p, d, rnd).start())

        def keep(p, rnd):
            pa[rnd, me] = bt[p]

        def part(q, o):
            return pltpu.make_async_remote_copy(
                ps.at[q, o - 1], pr.at[q, o - 1], p_send.at[q, o - 1], p_recv.at[q, o - 1],
                device_id={"harm": yside[o - 1]}, device_id_type=MESH)

        def gather_row(q, o):
            return pltpu.make_async_remote_copy(
                g[q].at[y], g[q].at[y], p_send.at[q, o - 1], p_recv.at[q, o - 1],
                device_id={"harm": yside[o - 1]}, device_id_type=MESH)

        def gather_row_arrived(q, o):
            src = (y + NY - o) % NY
            pltpu.make_async_remote_copy(
                g[q].at[src], g[q].at[src], p_send.at[q, o - 1], p_recv.at[q, o - 1],
                device_id={"harm": yside[o - 1]}, device_id_type=MESH).wait_recv()

        middle = (y == 1) | (y == 2) if FORWARD else False

        def gather_row_each(act):
            for o in range(1, NY):
                if FORWARD and o != 2:
                    pl.when(y != (3 if o == 1 else 0))(lambda o=o: act(o))
                else:
                    act(o)

        def handed(q):
            src = (y + 2) % NY
            return pltpu.make_async_remote_copy(
                g[q].at[src], g[q].at[src], f_send.at[q], p_recv.at[q, 2 * (y - 1)],
                device_id={"harm": (3 * (y - 1)) * NZ + z}, device_id_type=MESH)

        def hand_on(q):
            if FORWARD:
                @pl.when(middle)
                def _():
                    gather_row_arrived(q, 2)
                    handed(q).start()

        def ring_sum(q, way, hop):
            n = YSET.index(q)
            sign = 1 if (q + way) % 2 == 0 else -1
            buf, send, recv, hops = (ra, ra_send, ra_recv, HA) if way == 0 else (rb, rb_send, rb_recv, HB)
            away = (sign * (hops + 1 - hop)) % NZ
            src = cz.at[n, away - 1] if hop == 1 else buf.at[n, hop - 2]
            return pltpu.make_async_remote_copy(
                src, buf.at[n, hop - 1], send.at[n, hop - 1], recv.at[n, hop - 1],
                device_id={"harm": zside[0 if sign == 1 else 1]}, device_id_type=MESH)

        def ring_sum_step(q, way, hop):
            n = YSET.index(q)
            sign = 1 if (q + way) % 2 == 0 else -1
            buf, hops = (ra, HA) if way == 0 else (rb, HB)
            away = (sign * (hops + 1 - hop)) % NZ
            ring_sum(q, way, hop - 1).wait_recv()

            def one(i, _):
                for r in range(2):
                    for v in range(NVAR):
                        buf[n, hop - 2, i, r, v] = (
                            buf[n, hop - 2, i, r, v].astype(F32) + cz[n, away - 1, i, r, v].astype(F32)
                        ).astype(BF)
                return 0

            lax.fori_loop(0, 2, one, 0)
            ring_sum(q, way, hop).start()

        def out_copy(c):
            return pltpu.make_async_copy(ob.at[:, c], o_hbm.at[:, c], o_sem.at[c])

        def mixed(c):
            weights = [[mix[v, u] for u in range(NVAR)] for v in range(NVAR)]
            slots = [z if q in ZSET else y for q in (2 * c, 2 * c + 1)]

            def one(i, _):
                for r in range(2):
                    grads = []
                    for v in range(NVAR):
                        a = f[i, c, r, v].astype(F32)
                        prev = hr[0, c, i, v].astype(F32)
                        nxt = hr[1, c, i, v].astype(F32)
                        if r == 0:
                            prev = pltpu.roll(prev, 4, 0)
                        else:
                            nxt = pltpu.roll(nxt, 4, 0)
                        total = None
                        for s in range(1, 4):
                            up = pltpu.roll(jnp.where(row >= s, a, nxt), 8 - s, 0)
                            down = pltpu.roll(jnp.where(row < 8 - s, a, prev), s, 0)
                            right = pltpu.roll(a, 256 - s, 1)
                            left = pltpu.roll(a, s, 1)
                            piece = COEFFS[s - 1] * ((up - down) + (right - left))
                            total = piece if total is None else total + piece
                        grads.append(total)
                    for v in range(NVAR):
                        m = weights[v][0] * grads[0]
                        for u in range(1, NVAR):
                            m = m + weights[v][u] * grads[u]
                        m = m.astype(BF)
                        g[2 * c][slots[0], i, r, v] = m[:, :128]
                        g[2 * c + 1][slots[1], i, r, v] = m[:, 128:]
                return 0

            lax.fori_loop(0, 2, one, 0)

        shift = [hidx[j] & (NH - 1) for j in range(NBASE)]
        whole = [h // NT for h in shift]
        rest_of = [h % NT for h in shift]

        row1 = lax.broadcasted_iota(jnp.int32, (8, 128), 0)
        damp = jnp.zeros((8, 128), F32)
        for r in range(8):
            damp = jnp.where(row1 == r, -2.0 * flg[r].astype(F32), damp)

        def partial(q):
            c, half = q // 2, q % 2
            buf = g[q]

            def one(i, _):
                t = 2 * z + i
                k = y * NT + t
                freq = 0.1 * jnp.where(k < NH // 2, k, k - NH).astype(F32)
                pick = [(t + NT - b) % NT for b in rest_of]
                off = [(a + jnp.where(t < b, 1, 0)) % NY for a, b in zip(whole, rest_of)]
                hot = [[jnp.where(off[j] == o, 1.0, 0.0).astype(F32) for o in range(NY)] for j in range(NBASE)]
                for v in range(NVAR):
                    fre = f[i, c, 0, v, :, 128 * half : 128 * half + 128].astype(F32)
                    fim = f[i, c, 1, v, :, 128 * half : 128 * half + 128].astype(F32)
                    sums_re = [damp * fre - freq * fim] + [None] * NO
                    sums_im = [damp * fim + freq * fre] + [None] * NO
                    for j in range(NBASE):
                        mre = buf[pick[j] // 2, pick[j] % 2, 0, v].astype(F32)
                        mim = buf[pick[j] // 2, pick[j] % 2, 1, v].astype(F32)
                        bre = pb[2 * half * NVAR + v, j].astype(F32)
                        bim = pb[(2 * half + 1) * NVAR + v, j].astype(F32)
                        tre = bre * mre - bim * mim
                        tim = bre * mim + bim * mre
                        for o in range(NY):
                            if sums_re[o] is None:
                                sums_re[o] = hot[j][o] * tre
                                sums_im[o] = hot[j][o] * tim
                            else:
                                sums_re[o] = sums_re[o] + hot[j][o] * tre
                                sums_im[o] = sums_im[o] + hot[j][o] * tim
                    acc[q, i, 0, v] = sums_re[0]
                    acc[q, i, 1, v] = sums_im[0]
                    for o in range(1, NY):
                        ps[q, o - 1, i, 0, v] = sums_re[o].astype(BF)
                        ps[q, o - 1, i, 1, v] = sums_im[o].astype(BF)
                return 0

            lax.fori_loop(0, 2, one, 0)
            for o in range(1, NY):
                part(q, o).start()

        def shares(q):
            c, half = q // 2, q % 2
            n = YSET.index(q)
            buf = g[q]
            for o in range(1, NY):
                if FORWARD and o == 2:
                    pl.when(jnp.logical_not(middle))(lambda: gather_row_arrived(q, 2))
                else:
                    gather_row_arrived(q, o)

            def products(i, _):
                for j in range(NBASE):
                    t = (2 * z + i + rest_of[j]) % NT
                    src = (y + 2 * NY - whole[j] - jnp.where(t < rest_of[j], 1, 0)) % NY
                    for v in range(NVAR):
                        mre = buf[src, i, 0, v].astype(F32)
                        mim = buf[src, i, 1, v].astype(F32)
                        bre = pb[2 * half * NVAR + v, j].astype(F32)
                        bim = pb[(2 * half + 1) * NVAR + v, j].astype(F32)
                        prod[j, i, 0, v] = bre * mre - bim * mim
                        prod[j, i, 1, v] = bre * mim + bim * mre
                return 0

            lax.fori_loop(0, 2, products, 0)

            def taken(away, i):
                t = 2 * ((z + away) % NZ) + i
                out = []
                for j in range(NBASE):
                    u = (t + NT - rest_of[j]) % NT
                    out.append(jnp.where(u // 2 == z, u % 2, 2))
                return out

            def one(e, _):
                away, i = e // 2, e % 2
                idx = taken(away, i)
                for r in range(2):
                    for v in range(NVAR):
                        total = prod[0, idx[0], r, v] + prod[1, idx[1], r, v] + prod[2, idx[2], r, v]
                        cz[n, away - 1, i, r, v] = total.astype(BF)
                return 0

            first = (HA, HB if q % 2 else NZ - HB)
            for away in first:
                lax.fori_loop(2 * away, 2 * away + 2, one, 0)
            ring_sum(q, 0, 1).start()
            ring_sum(q, 1, 1).start()
            lo, hi = min(first), max(first) + 1
            lax.fori_loop(2, 2 * lo, one, 0)
            lax.fori_loop(2 * hi, 2 * NZ, one, 0)

            def here(i, _):
                idx = taken(0, i)
                k = y * NT + 2 * z + i
                freq = 0.1 * jnp.where(k < NH // 2, k, k - NH).astype(F32)
                for v in range(NVAR):
                    fre = f[i, c, 0, v, :, 128 * half : 128 * half + 128].astype(F32)
                    fim = f[i, c, 1, v, :, 128 * half : 128 * half + 128].astype(F32)
                    own_part = (damp * fre - freq * fim, damp * fim + freq * fre)
                    for r in range(2):
                        total = prod[0, idx[0], r, v] + prod[1, idx[1], r, v] + prod[2, idx[2], r, v]
                        acc[q, i, r, v] = own_part[r] + total
                return 0

            lax.fori_loop(0, 2, here, 0)

        def finish(q):
            c, half = q // 2, q % 2
            if q in ZSET:
                for o in range(1, NY):
                    part(q, o).wait_recv()
            else:
                ring_sum(q, 0, HA).wait_recv()
                ring_sum(q, 1, HB).wait_recv()

            def one(i, _):
                for r in range(2):
                    for v in range(NVAR):
                        total = acc[q, i, r, v]
                        if q in ZSET:
                            for o in range(1, NY):
                                total = total + pr[q, o - 1, i, r, v].astype(F32)
                        else:
                            n = YSET.index(q)
                            total = total + ra[n, HA - 1, i, r, v].astype(F32)
                            total = total + rb[n, HB - 1, i, r, v].astype(F32)
                        ob[i, c, r, v, :, 128 * half : 128 * half + 128] = total.astype(BF)
                return 0

            lax.fori_loop(0, 2, one, 0)
            if half == 1:
                out_copy(c).start()

        zero = jnp.zeros((8, 128), F32)
        for j in range(NBASE):
            for r in range(2):
                for v in range(NVAR):
                    prod[j, 2, r, v] = zero

        for c in range(NCOL):
            halo(0, c).start()
            halo(1, c).start()
            if c == 0:
                tiles_start()

        def relay(q, hop):
            if 1 <= hop <= HA:
                ring_arrived(q, 0, hop)
                if hop < HA:
                    ring(q, 0, hop + 1).start()
            if 1 <= hop <= HB:
                ring_arrived(q, 1, hop)
                if hop < HB:
                    ring(q, 1, hop + 1).start()

        for c in range(NCOL):
            halo(0, c).wait_recv()
            halo(1, c).wait_recv()
            mixed(c)
            for q in (2 * c, 2 * c + 1):
                if q in ZSET:
                    ring(q, 0, 1).start()
                    ring(q, 1, 1).start()
                else:
                    gather_row_each(lambda o, q=q: gather_row(q, o).start())
        for hop in range(1, HA):
            for q in ZSET:
                relay(q, hop)
            if hop == 1:
                collected(collect)
                for q in YSET[:2]:
                    hand_on(q)
            if hop == 2:
                for q in YSET[2:]:
                    hand_on(q)
        all_tiles(pb, u_recv.at[0])
        for n in range(2):
            for q in YSET[2 * n : 2 * n + 2]:
                shares(q)
            for q in ZSET[2 * n : 2 * n + 2 + n]:
                relay(q, HA)
                partial(q)
        for hop in range(2, HA + 1):
            for q in YSET:
                ring_sum_step(q, 0, hop)
                if hop <= HB:
                    ring_sum_step(q, 1, hop)
        for c in range(NCOL):
            halo(0, c).wait_send()
            halo(1, c).wait_send()
        for q in ZSET:
            for hop in range(1, HA + 1):
                ring(q, 0, hop).wait_send()
            for hop in range(1, HB + 1):
                ring(q, 1, hop).wait_send()
        all_tiles(bt, t_send.at[0])
        collected(lambda p, rnd: others(lambda d: tile_out(p, d, rnd).wait_send()))
        for q in YSET:
            gather_row_each(lambda o, q=q: gather_row(q, o).wait_send())
            if FORWARD:
                pl.when(middle)(lambda q=q: handed(q).wait_send())
            for hop in range(1, HA):
                ring_sum(q, 0, hop).wait_send()
                if hop < HB:
                    ring_sum(q, 1, hop).wait_send()
        for q in range(CHUNKS):
            finish(q)
        for q in ZSET:
            for o in range(1, NY):
                part(q, o).wait_send()
        for q in YSET:
            ring_sum(q, 0, HA).wait_send()
            ring_sum(q, 1, HB).wait_send()
        for c in range(NCOL):
            out_copy(c).wait()

    block = (2, 2, NVAR, 8, 128)
    dma = pltpu.SemaphoreType.DMA
    scratch = [
        pltpu.VMEM((2, NCOL, 2, NVAR, 8, 256), BF),
        pltpu.VMEM((2 * NVAR, 8, 256), BF),
        pltpu.VMEM((TILES, 8, 128), BF),
        pltpu.VMEM((2, NCOL, 2, NVAR, 8, 256), BF),
        pltpu.VMEM((2, NCOL, 2, NVAR, 8, 256), BF),
        pltpu.VMEM((ROUNDS, G, 8, 128), BF),
        pltpu.VMEM((TILES, NBASE, 8, 128), BF),
    ]
    scratch += [pltpu.VMEM((NZ if q in ZSET else NY,) + block, BF) for q in range(CHUNKS)]
    scratch += [
        pltpu.VMEM((CHUNKS, NO) + block, BF),
        pltpu.VMEM((CHUNKS, NO) + block, BF),
        pltpu.VMEM((CHUNKS,) + block, F32),
        pltpu.VMEM((2, NCOL, 2, NVAR, 8, 256), BF),
        dma((NCOL + 1,)),
        dma((2, NCOL)), dma((2, NCOL)),
        dma((CHUNKS, HA)), dma((CHUNKS, HA)),
        dma((CHUNKS, HB)), dma((CHUNKS, HB)),
        dma((1,)), dma((ROUNDS,)),
        dma((ROUNDS, G)), dma((1,)),
        dma((CHUNKS, NO)), dma((CHUNKS, NO)),
        dma((NCOL,)),
        pltpu.VMEM((NBASE, 3, 2, NVAR, 8, 128), F32),
        pltpu.VMEM((len(YSET), NZ - 1) + block, BF),
        pltpu.VMEM((len(YSET), HA) + block, BF),
        pltpu.VMEM((len(YSET), HB) + block, BF),
        dma((len(YSET), HA)), dma((len(YSET), HA)),
        dma((len(YSET), HB)), dma((len(YSET), HB)),
        dma((CHUNKS,)),
    ]
    smem = pl.BlockSpec(memory_space=pltpu.SMEM)
    hbm = pl.BlockSpec(memory_space=pl.ANY)

    def call(fields, base_store, harmonic_index, owners, sponge_flags, mixing):
        return pl.pallas_call(
            kernel,
            out_shape=jax.ShapeDtypeStruct(fields.shape, BF),
            in_specs=[hbm, hbm, smem, smem, smem, smem],
            out_specs=hbm,
            scratch_shapes=scratch,
            compiler_params=pltpu.CompilerParams(collective_id=0, has_side_effects=True),
            name="resolvent",
            interpret=interpret,
        )(fields, base_store.reshape(2 * NVAR, 8, 256), harmonic_index, owners, sponge_flags, mixing)

    return call


def wrap(mesh, call):
    return jax.shard_map(
        call,
        mesh=mesh,
        in_specs=(
            P("harm", None, None, None, "slab", None),
            P("harm", None, None, "slab", None),
            P(),
            P(),
            P("slab"),
            P(),
        ),
        out_specs=P("harm", None, None, None, "slab", None),
        check_vma=False,
    )


def solution(mesh):
    return wrap(mesh, build(4, mesh.shape["harm"] // 4, mesh.shape["slab"]))
```

```python
import jax
import jax.numpy as jnp
from jax import lax
from jax.experimental import pallas as pl
from jax.experimental.pallas import tpu as pltpu
from jax.sharding import PartitionSpec as P

COEFFS = (0.75, -0.15, 1.0 / 60.0)
NBASE = 3
NCOL = 4
NVAR = 5
CHUNKS = 8
COLLECT = 13
SPREAD = 5
MESH = pl.DeviceIdType.MESH
BF = jnp.bfloat16
F32 = jnp.float32


def build(NY, NZ, NS, interpret=False):
    NT = 2 * NZ
    NH = NY * NT
    HA = NZ // 2
    HB = NZ // 2 - 1
    NO = NY - 1
    G = NY * NZ
    TILES = 4 * NVAR
    ROUNDS = -(-TILES // G)
    FORWARD = NY == 4
    ZSET = (0, 1, 3, 4, 5)
    YSET = (2, 6, 7)

    def kernel(f_hbm, b_hbm, hidx, own, flg, mix, o_hbm, f, bown, bt, hs, hr, pa, pb, *rest):
        g = rest[:CHUNKS]
        (ps, pr, acc, ob, ld_sem, h_send, h_recv, a_send, a_recv, b_send, b_recv, t_send, t_recv, u_send, u_recv,
         p_send, p_recv, o_sem, prod, cz, ra, rb, ra_send, ra_recv, rb_send, rb_recv, f_send) = rest[CHUNKS:]
        me = lax.axis_index("harm")
        slab = lax.axis_index("slab")
        y, z = me // NZ, me % NZ
        zside = (y * NZ + (z + 1) % NZ, y * NZ + (z + NZ - 1) % NZ)
        yside = [((y + o) % NY) * NZ + z for o in range(1, NY)]
        sside = ((slab + 1) % NS, (slab + NS - 1) % NS)

        loads = [pltpu.make_async_copy(b_hbm, bown, ld_sem.at[NCOL])]
        loads += [pltpu.make_async_copy(f_hbm.at[:, c], f.at[:, c], ld_sem.at[c]) for c in range(NCOL)]
        for load in loads:
            load.start()

        def others(act):
            def one(o, _):
                act((me + o) % G)
                return 0

            lax.fori_loop(1, G, one, 0)

        barrier = pltpu.get_barrier_semaphore()
        others(lambda d: pl.semaphore_signal(barrier, inc=1, device_id={"harm": d}, device_id_type=MESH))
        for n in sside:
            pl.semaphore_signal(barrier, inc=1, device_id={"slab": n}, device_id_type=MESH)

        row = lax.broadcasted_iota(jnp.int32, (8, 256), 0)

        def pack(c):
            def one(i, _):
                for v in range(NVAR):
                    re = f[i, c, 0, v].astype(F32)
                    im = f[i, c, 1, v].astype(F32)
                    hs[0, c, i, v] = jnp.where(row < 4, pltpu.roll(re, 4, 0), im).astype(BF)
                    hs[1, c, i, v] = jnp.where(row < 4, re, pltpu.roll(im, 4, 0)).astype(BF)
                return 0

            lax.fori_loop(0, 2, one, 0)

        loads[0].wait()
        for half in range(2):
            for p in range(2 * NVAR):
                bt[2 * NVAR * half + p] = bown[p, :, 128 * half : 128 * half + 128]
        for c in range(NCOL):
            loads[1 + c].wait()
            pack(c)

        pl.semaphore_wait(barrier, G - 1 + 2)

        def halo(d, c):
            return pltpu.make_async_remote_copy(
                hs.at[d, c], hr.at[d, c], h_send.at[d, c], h_recv.at[d, c],
                device_id={"slab": sside[d]}, device_id_type=MESH)

        def ring(k, way, hop):
            sign = 1 if (k + way) % 2 == 0 else -1
            origin = (z + NZ - sign * (hop - 1)) % NZ
            buf = g[k]
            send, recv = (a_send, a_recv) if way == 0 else (b_send, b_recv)
            return pltpu.make_async_remote_copy(
                buf.at[origin], buf.at[origin], send.at[k, hop - 1], recv.at[k, hop - 1],
                device_id={"harm": zside[0 if sign == 1 else 1]}, device_id_type=MESH)

        def ring_arrived(k, way, hop):
            sign = 1 if (k + way) % 2 == 0 else -1
            origin = (z + NZ - sign * hop) % NZ
            buf = g[k]
            send, recv = (a_send, a_recv) if way == 0 else (b_send, b_recv)
            pltpu.make_async_remote_copy(
                buf.at[origin], buf.at[origin], send.at[k, hop - 1], recv.at[k, hop - 1],
                device_id={"harm": zside[0 if sign == 1 else 1]}, device_id_type=MESH).wait_recv()

        def tile_at(rnd):
            return SPREAD * me % G + rnd * G

        mine = sum(jnp.where(tile_at(rnd) < TILES, 1, 0) for rnd in range(ROUNDS))

        def tile_in(p):
            return pltpu.make_async_remote_copy(
                bt.at[p], pa.at[p // G, me], t_send.at[0], t_recv.at[p // G],
                device_id={"harm": COLLECT * p % G}, device_id_type=MESH)

        def tile_out(p, d, rnd):
            return pltpu.make_async_remote_copy(
                pb.at[p], pb.at[p], u_send.at[rnd, d], u_recv.at[0],
                device_id={"harm": d}, device_id_type=MESH)

        def bytes_of(ref, sem):
            pltpu.make_async_copy(ref, ref, sem).wait()

        def all_tiles(ref, sem):
            for n in range(ROUNDS + 1):
                pl.when(mine == n)(lambda n=n: bytes_of(ref.at[pl.ds(0, TILES - n)], sem))

        def tiles_start():
            for p in range(TILES):
                pl.when(COLLECT * p % G != me)(lambda p=p: tile_in(p).start())
            collected(keep)

        def collected(act):
            for rnd in range(ROUNDS):
                p = tile_at(rnd)
                pl.when(p < TILES)(lambda p=p, rnd=rnd: act(p, rnd))

        def collect(p, rnd):
            bytes_of(pa.at[rnd, pl.ds(0, G - 1)], t_recv.at[rnd])
            for j in range(NBASE):
                pb[p, j] = pa[rnd, own[j]]
            others(lambda d: tile_out(p, d, rnd).start())

        def keep(p, rnd):
            pa[rnd, me] = bt[p]

        def part(q, o):
            return pltpu.make_async_remote_copy(
                ps.at[q, o - 1], pr.at[q, o - 1], p_send.at[q, o - 1], p_recv.at[q, o - 1],
                device_id={"harm": yside[o - 1]}, device_id_type=MESH)

        def gather_row(q, o):
            return pltpu.make_async_remote_copy(
                g[q].at[y], g[q].at[y], p_send.at[q, o - 1], p_recv.at[q, o - 1],
                device_id={"harm": yside[o - 1]}, device_id_type=MESH)

        def gather_row_arrived(q, o):
            src = (y + NY - o) % NY
            pltpu.make_async_remote_copy(
                g[q].at[src], g[q].at[src], p_send.at[q, o - 1], p_recv.at[q, o - 1],
                device_id={"harm": yside[o - 1]}, device_id_type=MESH).wait_recv()

        middle = (y == 1) | (y == 2) if FORWARD else False

        def gather_row_each(act):
            for o in sorted(range(1, NY), key=lambda o: o != 2):
                if FORWARD and o != 2:
                    pl.when(y != (3 if o == 1 else 0))(lambda o=o: act(o))
                else:
                    act(o)

        def handed(q):
            src = (y + 2) % NY
            return pltpu.make_async_remote_copy(
                g[q].at[src], g[q].at[src], f_send.at[q], p_recv.at[q, 2 * (y - 1)],
                device_id={"harm": (3 * (y - 1)) * NZ + z}, device_id_type=MESH)

        def hand_on(q):
            if FORWARD:
                @pl.when(middle)
                def _():
                    gather_row_arrived(q, 2)
                    handed(q).start()

        def ring_sum(q, way, hop):
            n = YSET.index(q)
            sign = 1 if (q + way) % 2 == 0 else -1
            buf, send, recv, hops = (ra, ra_send, ra_recv, HA) if way == 0 else (rb, rb_send, rb_recv, HB)
            away = (sign * (hops + 1 - hop)) % NZ
            src = cz.at[n, away - 1] if hop == 1 else buf.at[n, hop - 2]
            return pltpu.make_async_remote_copy(
                src, buf.at[n, hop - 1], send.at[n, hop - 1], recv.at[n, hop - 1],
                device_id={"harm": zside[0 if sign == 1 else 1]}, device_id_type=MESH)

        def ring_sum_step(q, way, hop):
            n = YSET.index(q)
            sign = 1 if (q + way) % 2 == 0 else -1
            buf, hops = (ra, HA) if way == 0 else (rb, HB)
            away = (sign * (hops + 1 - hop)) % NZ
            ring_sum(q, way, hop - 1).wait_recv()

            def one(i, _):
                for r in range(2):
                    for v in range(NVAR):
                        buf[n, hop - 2, i, r, v] = (
                            buf[n, hop - 2, i, r, v].astype(F32) + cz[n, away - 1, i, r, v].astype(F32)
                        ).astype(BF)
                return 0

            lax.fori_loop(0, 2, one, 0)
            ring_sum(q, way, hop).start()

        def out_copy(c):
            return pltpu.make_async_copy(ob.at[:, c], o_hbm.at[:, c], o_sem.at[c])

        def mixed(c):
            weights = [[mix[v, u] for u in range(NVAR)] for v in range(NVAR)]
            slots = [z if q in ZSET else y for q in (2 * c, 2 * c + 1)]

            def one(i, _):
                for r in range(2):
                    grads = []
                    for v in range(NVAR):
                        a = f[i, c, r, v].astype(F32)
                        prev = hr[0, c, i, v].astype(F32)
                        nxt = hr[1, c, i, v].astype(F32)
                        if r == 0:
                            prev = pltpu.roll(prev, 4, 0)
                        else:
                            nxt = pltpu.roll(nxt, 4, 0)
                        total = None
                        for s in range(1, 4):
                            up = pltpu.roll(jnp.where(row >= s, a, nxt), 8 - s, 0)
                            down = pltpu.roll(jnp.where(row < 8 - s, a, prev), s, 0)
                            right = pltpu.roll(a, 256 - s, 1)
                            left = pltpu.roll(a, s, 1)
                            piece = COEFFS[s - 1] * ((up - down) + (right - left))
                            total = piece if total is None else total + piece
                        grads.append(total)
                    for v in range(NVAR):
                        m = weights[v][0] * grads[0]
                        for u in range(1, NVAR):
                            m = m + weights[v][u] * grads[u]
                        m = m.astype(BF)
                        g[2 * c][slots[0], i, r, v] = m[:, :128]
                        g[2 * c + 1][slots[1], i, r, v] = m[:, 128:]
                return 0

            lax.fori_loop(0, 2, one, 0)

        shift = [hidx[j] & (NH - 1) for j in range(NBASE)]
        whole = [h // NT for h in shift]
        rest_of = [h % NT for h in shift]

        row1 = lax.broadcasted_iota(jnp.int32, (8, 128), 0)
        damp = jnp.zeros((8, 128), F32)
        for r in range(8):
            damp = jnp.where(row1 == r, -2.0 * flg[r].astype(F32), damp)

        def partial(q):
            c, half = q // 2, q % 2
            buf = g[q]

            def one(i, _):
                t = 2 * z + i
                k = y * NT + t
                freq = 0.1 * jnp.where(k < NH // 2, k, k - NH).astype(F32)
                pick = [(t + NT - b) % NT for b in rest_of]
                off = [(a + jnp.where(t < b, 1, 0)) % NY for a, b in zip(whole, rest_of)]
                hot = [[jnp.where(off[j] == o, 1.0, 0.0).astype(F32) for o in range(NY)] for j in range(NBASE)]
                for v in range(NVAR):
                    fre = f[i, c, 0, v, :, 128 * half : 128 * half + 128].astype(F32)
                    fim = f[i, c, 1, v, :, 128 * half : 128 * half + 128].astype(F32)
                    sums_re = [damp * fre - freq * fim] + [None] * NO
                    sums_im = [damp * fim + freq * fre] + [None] * NO
                    for j in range(NBASE):
                        mre = buf[pick[j] // 2, pick[j] % 2, 0, v].astype(F32)
                        mim = buf[pick[j] // 2, pick[j] % 2, 1, v].astype(F32)
                        bre = pb[2 * half * NVAR + v, j].astype(F32)
                        bim = pb[(2 * half + 1) * NVAR + v, j].astype(F32)
                        tre = bre * mre - bim * mim
                        tim = bre * mim + bim * mre
                        for o in range(NY):
                            if sums_re[o] is None:
                                sums_re[o] = hot[j][o] * tre
                                sums_im[o] = hot[j][o] * tim
                            else:
                                sums_re[o] = sums_re[o] + hot[j][o] * tre
                                sums_im[o] = sums_im[o] + hot[j][o] * tim
                    acc[q, i, 0, v] = sums_re[0]
                    acc[q, i, 1, v] = sums_im[0]
                    for o in range(1, NY):
                        ps[q, o - 1, i, 0, v] = sums_re[o].astype(BF)
                        ps[q, o - 1, i, 1, v] = sums_im[o].astype(BF)
                return 0

            lax.fori_loop(0, 2, one, 0)
            @pl.when(y < NY // 2)
            def _():
                for o in range(NO, 0, -1):
                    part(q, o).start()

            @pl.when(y >= NY // 2)
            def _():
                for o in range(1, NY):
                    part(q, o).start()

        def shares(q):
            c, half = q // 2, q % 2
            n = YSET.index(q)
            buf = g[q]
            for o in range(1, NY):
                if FORWARD and o == 2:
                    pl.when(jnp.logical_not(middle))(lambda: gather_row_arrived(q, 2))
                else:
                    gather_row_arrived(q, o)

            def products(i, _):
                for j in range(NBASE):
                    t = (2 * z + i + rest_of[j]) % NT
                    src = (y + 2 * NY - whole[j] - jnp.where(t < rest_of[j], 1, 0)) % NY
                    for v in range(NVAR):
                        mre = buf[src, i, 0, v].astype(F32)
                        mim = buf[src, i, 1, v].astype(F32)
                        bre = pb[2 * half * NVAR + v, j].astype(F32)
                        bim = pb[(2 * half + 1) * NVAR + v, j].astype(F32)
                        prod[j, i, 0, v] = bre * mre - bim * mim
                        prod[j, i, 1, v] = bre * mim + bim * mre
                return 0

            lax.fori_loop(0, 2, products, 0)

            def taken(away, i):
                t = 2 * ((z + away) % NZ) + i
                out = []
                for j in range(NBASE):
                    u = (t + NT - rest_of[j]) % NT
                    out.append(jnp.where(u // 2 == z, u % 2, 2))
                return out

            def one(e, _):
                away, i = e // 2, e % 2
                idx = taken(away, i)
                for r in range(2):
                    for v in range(NVAR):
                        total = prod[0, idx[0], r, v] + prod[1, idx[1], r, v] + prod[2, idx[2], r, v]
                        cz[n, away - 1, i, r, v] = total.astype(BF)
                return 0

            first = (HA, HB if q % 2 else NZ - HB)
            for away in first:
                lax.fori_loop(2 * away, 2 * away + 2, one, 0)
            ring_sum(q, 0, 1).start()
            ring_sum(q, 1, 1).start()
            lo, hi = min(first), max(first) + 1
            lax.fori_loop(2, 2 * lo, one, 0)
            lax.fori_loop(2 * hi, 2 * NZ, one, 0)

            def here(i, _):
                idx = taken(0, i)
                k = y * NT + 2 * z + i
                freq = 0.1 * jnp.where(k < NH // 2, k, k - NH).astype(F32)
                for v in range(NVAR):
                    fre = f[i, c, 0, v, :, 128 * half : 128 * half + 128].astype(F32)
                    fim = f[i, c, 1, v, :, 128 * half : 128 * half + 128].astype(F32)
                    own_part = (damp * fre - freq * fim, damp * fim + freq * fre)
                    for r in range(2):
                        total = prod[0, idx[0], r, v] + prod[1, idx[1], r, v] + prod[2, idx[2], r, v]
                        acc[q, i, r, v] = own_part[r] + total
                return 0

            lax.fori_loop(0, 2, here, 0)

        def finish(q):
            c, half = q // 2, q % 2
            if q in ZSET:
                for o in range(1, NY):
                    part(q, o).wait_recv()
            else:
                ring_sum(q, 0, HA).wait_recv()
                ring_sum(q, 1, HB).wait_recv()

            def one(i, _):
                for r in range(2):
                    for v in range(NVAR):
                        total = acc[q, i, r, v]
                        if q in ZSET:
                            for o in range(1, NY):
                                total = total + pr[q, o - 1, i, r, v].astype(F32)
                        else:
                            n = YSET.index(q)
                            total = total + ra[n, HA - 1, i, r, v].astype(F32)
                            total = total + rb[n, HB - 1, i, r, v].astype(F32)
                        ob[i, c, r, v, :, 128 * half : 128 * half + 128] = total.astype(BF)
                return 0

            lax.fori_loop(0, 2, one, 0)
            if half == 1:
                out_copy(c).start()

        zero = jnp.zeros((8, 128), F32)
        for j in range(NBASE):
            for r in range(2):
                for v in range(NVAR):
                    prod[j, 2, r, v] = zero

        for c in range(NCOL):
            halo(0, c).start()
            halo(1, c).start()
            if c == 0:
                tiles_start()

        def relay(q, hop):
            if 1 <= hop <= HA:
                ring_arrived(q, 0, hop)
                if hop < HA:
                    ring(q, 0, hop + 1).start()
            if 1 <= hop <= HB:
                ring_arrived(q, 1, hop)
                if hop < HB:
                    ring(q, 1, hop + 1).start()

        for c in range(NCOL):
            halo(0, c).wait_recv()
            halo(1, c).wait_recv()
            mixed(c)
            for q in (2 * c, 2 * c + 1):
                if q in ZSET:
                    ring(q, 0, 1).start()
                    ring(q, 1, 1).start()
                else:
                    gather_row_each(lambda o, q=q: gather_row(q, o).start())
        for hop in range(1, HA):
            for q in ZSET:
                relay(q, hop)
            if hop == 1:
                collected(collect)
                for q in YSET[:2]:
                    hand_on(q)
            if hop == 2:
                for q in YSET[2:]:
                    hand_on(q)
        all_tiles(pb, u_recv.at[0])
        for n in range(2):
            for q in YSET[2 * n : 2 * n + 2]:
                shares(q)
            for q in ZSET[2 * n : 2 * n + 2 + n]:
                relay(q, HA)
                partial(q)
        for hop in range(2, HA + 1):
            for q in YSET:
                ring_sum_step(q, 0, hop)
                if hop <= HB:
                    ring_sum_step(q, 1, hop)
        for c in range(NCOL):
            halo(0, c).wait_send()
            halo(1, c).wait_send()
        for q in ZSET:
            for hop in range(1, HA + 1):
                ring(q, 0, hop).wait_send()
            for hop in range(1, HB + 1):
                ring(q, 1, hop).wait_send()
        all_tiles(bt, t_send.at[0])
        collected(lambda p, rnd: others(lambda d: tile_out(p, d, rnd).wait_send()))
        for q in YSET:
            gather_row_each(lambda o, q=q: gather_row(q, o).wait_send())
            if FORWARD:
                pl.when(middle)(lambda q=q: handed(q).wait_send())
            for hop in range(1, HA):
                ring_sum(q, 0, hop).wait_send()
                if hop < HB:
                    ring_sum(q, 1, hop).wait_send()
        for q in range(CHUNKS):
            finish(q)
        for q in ZSET:
            for o in range(1, NY):
                part(q, o).wait_send()
        for q in YSET:
            ring_sum(q, 0, HA).wait_send()
            ring_sum(q, 1, HB).wait_send()
        for c in range(NCOL):
            out_copy(c).wait()

    block = (2, 2, NVAR, 8, 128)
    dma = pltpu.SemaphoreType.DMA
    scratch = [
        pltpu.VMEM((2, NCOL, 2, NVAR, 8, 256), BF),
        pltpu.VMEM((2 * NVAR, 8, 256), BF),
        pltpu.VMEM((TILES, 8, 128), BF),
        pltpu.VMEM((2, NCOL, 2, NVAR, 8, 256), BF),
        pltpu.VMEM((2, NCOL, 2, NVAR, 8, 256), BF),
        pltpu.VMEM((ROUNDS, G, 8, 128), BF),
        pltpu.VMEM((TILES, NBASE, 8, 128), BF),
    ]
    scratch += [pltpu.VMEM((NZ if q in ZSET else NY,) + block, BF) for q in range(CHUNKS)]
    scratch += [
        pltpu.VMEM((CHUNKS, NO) + block, BF),
        pltpu.VMEM((CHUNKS, NO) + block, BF),
        pltpu.VMEM((CHUNKS,) + block, F32),
        pltpu.VMEM((2, NCOL, 2, NVAR, 8, 256), BF),
        dma((NCOL + 1,)),
        dma((2, NCOL)), dma((2, NCOL)),
        dma((CHUNKS, HA)), dma((CHUNKS, HA)),
        dma((CHUNKS, HB)), dma((CHUNKS, HB)),
        dma((1,)), dma((ROUNDS,)),
        dma((ROUNDS, G)), dma((1,)),
        dma((CHUNKS, NO)), dma((CHUNKS, NO)),
        dma((NCOL,)),
        pltpu.VMEM((NBASE, 3, 2, NVAR, 8, 128), F32),
        pltpu.VMEM((len(YSET), NZ - 1) + block, BF),
        pltpu.VMEM((len(YSET), HA) + block, BF),
        pltpu.VMEM((len(YSET), HB) + block, BF),
        dma((len(YSET), HA)), dma((len(YSET), HA)),
        dma((len(YSET), HB)), dma((len(YSET), HB)),
        dma((CHUNKS,)),
    ]
    smem = pl.BlockSpec(memory_space=pltpu.SMEM)
    hbm = pl.BlockSpec(memory_space=pl.ANY)

    def call(fields, base_store, harmonic_index, owners, sponge_flags, mixing):
        return pl.pallas_call(
            kernel,
            out_shape=jax.ShapeDtypeStruct(fields.shape, BF),
            in_specs=[hbm, hbm, smem, smem, smem, smem],
            out_specs=hbm,
            scratch_shapes=scratch,
            compiler_params=pltpu.CompilerParams(collective_id=0, has_side_effects=True),
            name="resolvent",
            interpret=interpret,
        )(fields, base_store.reshape(2 * NVAR, 8, 256), harmonic_index, owners, sponge_flags, mixing)

    return call


def wrap(mesh, call):
    return jax.shard_map(
        call,
        mesh=mesh,
        in_specs=(
            P("harm", None, None, None, "slab", None),
            P("harm", None, None, "slab", None),
            P(),
            P(),
            P("slab"),
            P(),
        ),
        out_specs=P("harm", None, None, None, "slab", None),
        check_vma=False,
    )


def solution(mesh):
    return wrap(mesh, build(4, mesh.shape["harm"] // 4, mesh.shape["slab"]))
```
